256 devices in a mesh: seq: 16 (over y_hi, x, core), dp: 16 (over y_lo, z).
Axes of the slice: x: 4, y: 4 (y_hi: 2, y_lo: 2; y = y_hi * 2 + y_lo), z: 8, core: 2. Of those that a mesh axis runs over, the one named last changes fastest.
Arguments:
- query: bfloat16 [16, 3072, 1280], P('dp', 'seq'), may hold values from -52 to 52, as said below
- keys: bfloat16 [16, 3072, 1280], P('dp', 'seq'), may hold values from -6 to 6, as said below
- values: bfloat16 [16, 3072, 1280], P('dp', 'seq'), may hold values from -6 to 6
- attn: bfloat16 [16, 3072, 1280], P('dp', 'seq'), may hold values from -6 to 6
- d_block: bfloat16 [16, 3072, 1280], P('dp', 'seq'), may hold values from -6 to 6
- w_out: bfloat16 [1280, 1280], P('dp'), may hold values from -0.15625 to 0.15625
Outputs:
- d_query: bfloat16 [16, 3072, 1280], P('dp', 'seq')
- d_keys: bfloat16 [16, 3072, 1280], P('dp', 'seq')
- d_values: bfloat16 [16, 3072, 1280], P('dp', 'seq')
- d_weight: float32 [1280, 1280], P('dp')
The draws below stay inside these ranges and needn't reach their ends.
Inputs may be any that keep to these rules, and one draw needn't show every extreme that they name: Some query patches may lie along the sum of two keys of the same video. keys has entries of order one.
All inputs are finite; a program needn't handle non-finite values.
Results may differ from the reference program's by a relative error of at most 0.0058.
Values may be sent and summed in bfloat16 or wider, within the bound.
No kernel may reach another device: no remote copies, remote signals or barrier semaphores. Data moves between devices by JAX's collectives and lax.ppermute only.
A program may use at most 64 MiB of HBM per device.

```python
import jax
import jax.numpy as jnp
from jax import lax

HEADS = 16
HEAD_DIM = 80
D = 1280
PATCHES = 3072
VIDEOS = 16


def shared_pair(key):
    shape_all = (VIDEOS, PATCHES, HEADS * HEAD_DIM)
    keys_raw = jnp.clip(jax.random.normal(jax.random.fold_in(key, 101), shape_all, jnp.float32), -6.0, 6.0)
    query_raw = jnp.clip(jax.random.normal(jax.random.fold_in(key, 202), shape_all, jnp.float32), -6.0, 6.0)
    keys_out = keys_raw
    query_out = query_raw
    return (query_out, keys_out)


def draw_query(key, part):
    return shared_pair(key)[0].astype(jnp.bfloat16)


def draw_keys(key, part):
    return shared_pair(key)[1].astype(jnp.bfloat16)


def raised(entries, own_key, source, target, parts, factor):
    owner, partner = [(jnp.arange(entries.shape[axis_at]) // (entries.shape[axis_at] // parts)).reshape([-1 if axis == axis_at else 1 for axis in range(entries.ndim)]) for axis_at in (source, target)]
    chosen = jax.random.permutation(own_key, parts)[partner]
    strong = (owner == chosen) | (owner == (partner + parts // 2) % parts)
    return jnp.where(strong, factor * entries, entries)


def block_scale(rng, shape, shards, low, top_value):
    gain, own = 1.0, jax.random.fold_in(rng, 6)
    for position, shards_of in shards:
        steps = jnp.exp(jax.random.uniform(jax.random.fold_in(own, position), (shards_of,), jnp.float32, low / len(shards), top_value / len(shards)))
        gain = gain * jnp.repeat(steps, shape[position] // shards_of).reshape([-1 if axis == position else 1 for axis in range(len(shape))])
    return gain


def noise(key, shape, deviation, limit, shards=(), kind=jnp.bfloat16):
    values = deviation * jax.random.normal(key, shape, jnp.float32)
    if shards:
        values = values * block_scale(key, shape, shards, -0.22, 0.18)
    return jnp.clip(values, -limit, limit).astype(kind)


def noise_with(rng, extent, width, reach, shards, heavy, held_as=jnp.bfloat16):
    drawn = width * jax.random.normal(rng, extent, jnp.float32)
    if shards:
        drawn = drawn * block_scale(rng, extent, shards, -0.22, 0.18)
    return jnp.clip(raised(drawn, jax.random.fold_in(rng, 3), *heavy), -reach, reach).astype(held_as)


def setup_inputs(seed: int = 0) -> dict:
    seeds = jax.random.split(jax.random.key(seed), 7)
    query = draw_query(jax.random.fold_in(seeds[6], 71), 0)
    keys = draw_keys(jax.random.fold_in(seeds[6], 71), 0)
    values = noise(seeds[2], (VIDEOS, PATCHES, D), 1.0, 6.0, ((0, 16), (1, 16)))
    attn = noise_with(seeds[3], (VIDEOS, PATCHES, D), 1.0, 6.0, ((0, 16), (1, 16)), (1, 2, 16, 2.0))
    d_block = noise(seeds[4], (VIDEOS, PATCHES, D), 1.0, 6.0, ((0, 16), (1, 16)))
    w_out = noise(seeds[5], (D, D), D ** -0.5, 0.15625, ((0, 16),))
    return dict(query=query, keys=keys, values=values, attn=attn, d_block=d_block, w_out=w_out)


def head_gradients(item):
    query_h, keys_h, values_h, dout_h, delta_h = item
    score_scale = HEAD_DIM ** -0.5
    scores = jnp.dot(query_h, keys_h.T, preferred_element_type=jnp.float32) * score_scale
    row_max = jnp.max(scores, axis=1, keepdims=True)
    lse = row_max + jnp.log(jnp.sum(jnp.exp(scores - row_max), axis=1, keepdims=True))
    probs = jnp.exp(scores - lse)
    probs_low = probs.astype(jnp.bfloat16)
    d_values = jnp.dot(probs_low.T, dout_h, preferred_element_type=jnp.float32)
    d_probs = jnp.dot(dout_h, values_h.T, preferred_element_type=jnp.float32)
    d_scores = (score_scale * probs * (d_probs - delta_h[:, None])).astype(jnp.bfloat16)
    d_query = jnp.dot(d_scores, keys_h, preferred_element_type=jnp.float32)
    d_keys = jnp.dot(d_scores.T, query_h, preferred_element_type=jnp.float32)
    return (d_query.astype(jnp.bfloat16), d_keys.astype(jnp.bfloat16), d_values.astype(jnp.bfloat16))


def reference(query, keys, values, attn, d_block, w_out):
    features = HEADS * HEAD_DIM
    grad_y = d_block.reshape(VIDEOS * PATCHES, features)
    attn_rows = attn.reshape(VIDEOS * PATCHES, features)
    d_out = jnp.dot(grad_y, w_out.T, preferred_element_type=jnp.float32).astype(jnp.bfloat16)
    delta = jnp.sum((d_out.astype(jnp.float32) * attn_rows.astype(jnp.float32)).reshape(VIDEOS, PATCHES, HEADS, HEAD_DIM), axis=3)

    def by_head(array):
        return array.reshape(VIDEOS, PATCHES, HEADS, HEAD_DIM).transpose(0, 2, 1, 3).reshape(VIDEOS * HEADS, PATCHES, HEAD_DIM)

    delta_heads = delta.transpose(0, 2, 1).reshape(VIDEOS * HEADS, PATCHES)
    d_query, d_keys, d_values = lax.map(head_gradients, (by_head(query), by_head(keys), by_head(values), by_head(d_out.reshape(VIDEOS, PATCHES, features)), delta_heads))

    def by_patch(array):
        return array.reshape(VIDEOS, HEADS, PATCHES, HEAD_DIM).transpose(0, 2, 1, 3).reshape(VIDEOS, PATCHES, features)

    total = jnp.dot(attn_rows.T, grad_y, preferred_element_type=jnp.float32)
    d_weight = total * (1.0 / (float(VIDEOS * PATCHES) ** 0.5))
    return (by_patch(d_query), by_patch(d_keys), by_patch(d_values), d_weight)
```

```python
import functools

import jax
import jax.numpy as jnp
from jax import lax
from jax.experimental import pallas as pl
from jax.experimental.pallas import tpu as pltpu
from jax.sharding import Mesh
from jax.sharding import PartitionSpec as P

BF = jnp.bfloat16
F32 = jnp.float32
HD = 80
HALF = 40
HEADS = 16
SRC = 16
N = 3072
TOK = 192
BIG = 128
SMALL = 64
EXT = 96
D = 1280
SCALE = HD**-0.5
LOG2E = 1.4426950408889634
VMEM_LIMIT = 56 * 1024 * 1024
SEQ = ("yh", "x", "c")
DP = ("yl", "z")
OFFSETS = (0, -1, 1, -2, 2, -3, 3, -4)


def params(limit=VMEM_LIMIT):
    return pltpu.CompilerParams(vmem_limit_bytes=limit)


def cost(flops, read, exps=0):
    return pl.CostEstimate(flops=flops, bytes_accessed=read, transcendentals=exps)


def whole(*shape):
    return pl.BlockSpec(shape, lambda *_: (0,) * len(shape))


def dot(a, b, ca, cb):
    return lax.dot_general(a, b, (((ca,), (cb,)), ((), ())), preferred_element_type=F32)


def lanes3(a, b):
    return jnp.concatenate([a[:, :BIG], b[:, :BIG], a[:, BIG:], b[:, BIG:]], axis=1)


def pack_qkv_body(q_ref, k_ref, v_ref, out_ref):
    qt, kt, vt = q_ref[0].T, k_ref[0].T, v_ref[0].T
    for h in range(HEADS):
        a = h * HD
        out_ref[h, 0:HD, :] = lanes3(qt[a : a + HD], kt[a : a + HD])
        v = vt[a : a + HD].astype(F32)
        out_ref[h, HD : HD + HALF, :] = lanes3(v[:HALF], v[HALF:]).astype(BF)


def pack_qkv(q, k, v):
    return pl.pallas_call(
        pack_qkv_body,
        out_shape=jax.ShapeDtypeStruct((HEADS, HD + HALF, 384), BF),
        compiler_params=params(),
        cost_estimate=cost(0, 3 * 10**6),
        name="pack_qkv",
    )(q, k, v)


def split_attn_body(c_ref, a_ref, own_ref, send_ref, at):
    at[...] = a_ref[0].T.astype(F32)
    c = c_ref[0]
    for h in range(HEADS):
        keep = pl.multiple_of(h * HD + c * HALF, 8)
        give = pl.multiple_of(h * HD + (1 - c) * HALF, 8)
        own_ref[h] = at[pl.ds(keep, HALF), :].astype(BF)
        send_ref[h] = at[pl.ds(give, HALF), :].astype(BF)


def split_attn(c, attn):
    vm = pl.BlockSpec(memory_space=pltpu.VMEM)
    shape = jax.ShapeDtypeStruct((HEADS, HALF, TOK), BF)
    return pl.pallas_call(
        split_attn_body,
        in_specs=[pl.BlockSpec(memory_space=pltpu.SMEM), vm],
        out_specs=[vm, vm],
        out_shape=[shape, shape],
        scratch_shapes=[pltpu.VMEM((D, TOK), F32)],
        compiler_params=params(),
        cost_estimate=cost(0, 10**6),
        name="split_attn",
    )(c, attn)


def weight_share_body(y_ref, g_own, g_oth, a_own, a_oth, keep_ref, give_ref, gx_ref, ax_ref, acc):
    gx_ref[0:128] = g_own[0, 0:128]
    gx_ref[128:256] = g_oth[0, 0:128]
    gx_ref[256:320] = g_own[0, 128:192]
    gx_ref[320:384] = g_oth[0, 128:192]
    for h in range(HEADS):
        ax_ref[h] = lanes3(a_own[h].astype(F32), a_oth[h].astype(F32)).astype(BF)
    rows = jnp.concatenate([ax_ref[h].astype(F32) for h in range(HEADS)], axis=0).astype(BF)
    acc[...] = dot(rows, gx_ref[...], 1, 0)
    y = y_ref[0]
    for k in range(8):
        keep = pl.multiple_of((y * 8 + k) * HALF, 8)
        give = pl.multiple_of(((1 - y) * 8 + k) * HALF, 8)
        keep_ref[k] = acc[pl.ds(keep, HALF), :].astype(BF)
        give_ref[k] = acc[pl.ds(give, HALF), :].astype(BF)


def weight_share(y, g_own, g_oth, a_own, a_oth):
    vm = pl.BlockSpec(memory_space=pltpu.VMEM)
    return pl.pallas_call(
        weight_share_body,
        in_specs=[pl.BlockSpec(memory_space=pltpu.SMEM)] + [vm] * 4,
        out_specs=[vm] * 4,
        out_shape=[
            jax.ShapeDtypeStruct((8, HALF, D), BF),
            jax.ShapeDtypeStruct((8, HALF, D), BF),
            jax.ShapeDtypeStruct((384, D), BF),
            jax.ShapeDtypeStruct((HEADS, HALF, 384), BF),
        ],
        scratch_shapes=[pltpu.VMEM((640, D), F32)],
        compiler_params=params(),
        cost_estimate=cost(2 * 640 * 384 * D, 6 * 10**6),
        name="weight_share",
    )(y, g_own, g_oth, a_own, a_oth)


def sum_z_body(x_ref, out_ref):
    t = x_ref[0].astype(F32)
    for k in range(1, 8):
        t = t + x_ref[k].astype(F32)
    pad = jnp.zeros((7, 128), F32)
    for g in range(8):
        rows = t[5 * g : 5 * g + 5]
        for half in range(2):
            a = half * 640
            p = jnp.concatenate([rows[:, a + 128 * j : a + 128 * j + 128] for j in range(5)] + [pad], axis=0)
            out_ref[2 * g + half] = jnp.concatenate([p[:16], p[16:]], axis=1).astype(BF)


def sum_z(x):
    return pl.pallas_call(
        sum_z_body,
        out_shape=jax.ShapeDtypeStruct((SRC, 16, 256), BF),
        compiler_params=params(),
        cost_estimate=cost(0, 10**6),
        name="sum_z",
    )(x)


def sum_seq_body(x_ref, out_ref):
    halves = []
    for c in range(2):
        t = x_ref[c].astype(F32)
        for k in range(1, 8):
            t = t + x_ref[2 * k + c].astype(F32)
        halves.append(jnp.concatenate([t[:, :128], t[:9, 128:]], axis=0))
    t = jnp.concatenate(halves + [jnp.zeros((6, 128), F32)], axis=0) * (1.0 / float(16 * N) ** 0.5)
    low = t.astype(BF)
    for s in range(SRC):
        out_ref[s] = low


def sum_seq(x):
    return pl.pallas_call(
        sum_seq_body,
        out_shape=jax.ShapeDtypeStruct((SRC, 56, 128), BF),
        compiler_params=params(),
        cost_estimate=cost(0, 10**6),
        name="sum_seq",
    )(x)


def out_grad_body(ids, *refs):
    w_refs, (gx_ref, ax_ref, out_ref, w, acc) = refs[:8], refs[8:]
    for r in range(8):
        both = jnp.concatenate([w_refs[r][0].astype(F32), w_refs[r][1].astype(F32)], axis=0)
        w[r * HD : (r + 1) * HD] = both.astype(BF)
    acc[...] = dot(w[...], gx_ref[...], 1, 1)
    for r in range(HEADS):
        h = ids[r]
        low = acc[r * HALF : (r + 1) * HALF].astype(BF).astype(F32)
        minus = -jnp.sum(low * ax_ref[h].astype(F32), axis=0, keepdims=True)
        p1 = minus.astype(BF).astype(F32)
        p2 = (minus - p1).astype(BF).astype(F32)
        p3 = minus - p1 - p2
        pad = jnp.zeros((5, 384), F32)
        out_ref[h] = jnp.concatenate([low, p1, p2, p3, pad], axis=0).astype(BF)


def out_grad(ids, blocks, gx, ax):
    vm = pl.BlockSpec(memory_space=pltpu.VMEM)
    return pl.pallas_call(
        out_grad_body,
        in_specs=[pl.BlockSpec(memory_space=pltpu.SMEM)] + [vm] * 10,
        out_specs=vm,
        out_shape=jax.ShapeDtypeStruct((HEADS, 48, 384), BF),
        scratch_shapes=[pltpu.VMEM((640, D), BF), pltpu.VMEM((640, 384), F32)],
        compiler_params=params(),
        cost_estimate=cost(2 * 640 * 384 * D, 4 * 10**6),
        name="out_grad",
    )(ids, *blocks, gx, ax)


def each_place(put):
    for s in range(SRC):
        put(s * BIG, ((s, 0),))
    for s in range(0, SRC, 2):
        put(SRC * BIG + s * SMALL, ((s, 1), (s + 1, 1)))


def piece(x_ref, s, rows, col, small):
    if small:
        a = 2 * BIG + col * SMALL
        return x_ref[s, rows, a : a + SMALL]
    return x_ref[s, rows, col * BIG : (col + 1) * BIG]


def joined(parts):
    return parts[0] if len(parts) == 1 else jnp.concatenate(parts, axis=1)


def score_half(kn, q, s_new, s_old, m_old, emit, chunk, cols):
    m = jnp.full((8, cols), -jnp.inf, F32)
    total = jnp.zeros((8, cols), F32)
    for r in range(0, N, chunk):
        if q is not None:
            s = dot(kn[r : r + chunk, :], q, 1, 0)
            s_new[r : r + chunk, :] = s
            m = jnp.maximum(m, jnp.max(s.reshape(chunk // 8, 8, cols), axis=0))
        if s_old is not None:
            e = jnp.exp2((s_old[r : r + chunk, :] - m_old) * (SCALE * LOG2E))
            total = total + jnp.sum(e.reshape(chunk // 8, 8, cols), axis=0)
            emit(r, e.astype(BF))
    return jnp.max(m, axis=0, keepdims=True), jnp.sum(total, axis=0, keepdims=True)


def scores_body(cols, chunk, x_ref, e_ref, inv_ref, qn_ref, kt_ref, vn_ref, qt, kn, sa, sb, ma):
    i = pl.program_id(0)
    blocks = N // cols

    @pl.when(i == 0)
    def _():
        ones = jnp.concatenate([jnp.ones((8, 128), F32), jnp.zeros((8, 128), F32)], axis=0)

        def put(a, pieces):
            q = joined([piece(x_ref, s, slice(0, HD), 0, small) for s, small in pieces])
            k = joined([piece(x_ref, s, slice(0, HD), 1, small) for s, small in pieces])
            qt[:, a : a + 128] = q
            qn_ref[a : a + 128, :] = q.T
            kt_ref[:, a : a + 128] = k
            kn[a : a + 128, :] = k.T
            rows = slice(HD, HD + HALF)
            low = joined([piece(x_ref, s, rows, 0, small).astype(F32) for s, small in pieces])
            high = joined([piece(x_ref, s, rows, 1, small).astype(F32) for s, small in pieces])
            v = jnp.concatenate([low, high, ones], axis=0)
            vn_ref[a : a + 128, :] = v.T.astype(BF)

        each_place(put)
        m, _ = score_half(kn, qt[:, 0:cols], sa, None, None, None, chunk, cols)
        ma[...] = jnp.broadcast_to(m, ma.shape)

    def q_block(b):
        return qt[:, pl.ds(pl.multiple_of(b * cols, cols), cols)]

    def emit0(r, v):
        e_ref[r : r + chunk, 0:cols] = v

    def emit1(r, v):
        e_ref[r : r + chunk, cols : 2 * cols] = v

    mb, l0 = score_half(kn, q_block(2 * i + 1), sb, sa, ma[0:1, :], emit0, chunk, cols)
    nxt = jnp.minimum(2 * i + 2, blocks - 1)
    mn, l1 = score_half(kn, q_block(nxt), sa, sb, mb, emit1, chunk, cols)
    ma[...] = jnp.broadcast_to(mn, ma.shape)
    inv_ref[...] = jnp.broadcast_to(1.0 / jnp.concatenate([l0, l1], axis=1), (8, 2 * cols))


def scores(qkv, cols=256, chunk=128):
    return pl.pallas_call(
        functools.partial(scores_body, cols, chunk),
        grid=(N // cols // 2,),
        in_specs=[whole(SRC, HD + HALF, 384)],
        out_specs=[
            pl.BlockSpec((N, 2 * cols), lambda i: (0, i)),
            pl.BlockSpec((8, 2 * cols), lambda i: (0, i)),
            whole(N, HD),
            whole(HD, N),
            whole(N, EXT),
        ],
        out_shape=[
            jax.ShapeDtypeStruct((N, N), BF),
            jax.ShapeDtypeStruct((8, N), F32),
            jax.ShapeDtypeStruct((N, HD), BF),
            jax.ShapeDtypeStruct((HD, N), BF),
            jax.ShapeDtypeStruct((N, EXT), BF),
        ],
        scratch_shapes=[
            pltpu.VMEM((HD, N), BF),
            pltpu.VMEM((N, HD), BF),
            pltpu.VMEM((N, cols), F32),
            pltpu.VMEM((N, cols), F32),
            pltpu.VMEM((8, cols), F32),
        ],
        compiler_params=params(),
        cost_estimate=cost(2 * N * N * HD, 24 * 10**6, N * N),
        name="scores",
    )(qkv)


def grads_block(k0, rows, e_ref, inv_ref, qn_ref, kt_ref, vn, dot_t, dot_n, acc):
    e = e_ref[...]
    dp = dot(vn[pl.ds(k0, rows), :], dot_t[...], 1, 0)
    ds = (e.astype(F32) * dp * inv_ref[0:1, :]).astype(BF)
    dv = dot(e, dot_n[...], 1, 0)
    dk = dot(ds, qn_ref[...], 1, 0) * SCALE
    acc[...] += dot(kt_ref[:, pl.ds(k0, rows)], ds, 1, 0)
    return dv.T.astype(BF), dk.T.astype(BF)


def grads_a_body(rows, x_ref, e_ref, inv_ref, qn_ref, kt_ref, vn_ref, out_ref, dq_ref, dot_t, dot_n):
    i = pl.program_id(0)

    @pl.when(i == 0)
    def _():
        def side(s, small, sl):
            own = piece(x_ref, s, sl, 0, small).astype(F32)
            other = piece(x_ref, s ^ 1, sl, 1, small).astype(F32)
            return own, other

        def put(a, pieces):
            feats = []
            sums = []
            for s, small in pieces:
                own, other = side(s, small, slice(0, 48))
                first, second = (own, other) if s % 2 == 0 else (other, own)
                feats.append(jnp.concatenate([first[:HALF], second[:HALF]], axis=0))
                sums.append(own[HALF:] + jnp.concatenate([jnp.zeros((3, own.shape[1]), F32), other[HALF : HALF + 3], jnp.zeros((2, own.shape[1]), F32)], axis=0))
            f = joined(feats)
            t = joined(sums)
            dot_t[:, a : a + 128] = jnp.concatenate([f, t, jnp.zeros((8, 128), F32)], axis=0).astype(BF)
            dot_n[a : a + 128, :] = (f * inv_ref[0:1, a : a + 128]).T.astype(BF)

        each_place(put)
        dq_ref[...] = jnp.zeros_like(dq_ref)

    k0 = pl.multiple_of(i * rows, 128)
    dv, dk = grads_block(k0, rows, e_ref, inv_ref, qn_ref, kt_ref, vn_ref, dot_t, dot_n, dq_ref)
    for j in range(rows // BIG):
        out_ref[j, 0:HD, 0:BIG] = dv[:, j * BIG : (j + 1) * BIG]
        out_ref[j, 0:HD, BIG : 2 * BIG] = dk[:, j * BIG : (j + 1) * BIG]


def grads_a(dout, e, inv, qn, kt, vn, rows=256):
    return pl.pallas_call(
        functools.partial(grads_a_body, rows),
        grid=(SRC * BIG // rows,),
        in_specs=[
            whole(SRC, 48, 384),
            pl.BlockSpec((rows, N), lambda i: (i, 0)),
            whole(8, N),
            whole(N, HD),
            whole(HD, N),
            whole(N, EXT),
        ],
        out_specs=[
            pl.BlockSpec((rows // BIG, HD + 16, 2 * BIG), lambda i: (i, 0, 0)),
            whole(HD, N),
            whole(EXT, N),
            whole(N, HD),
        ],
        out_shape=[
            jax.ShapeDtypeStruct((SRC, HD + 16, 2 * BIG), BF),
            jax.ShapeDtypeStruct((HD, N), F32),
            jax.ShapeDtypeStruct((EXT, N), BF),
            jax.ShapeDtypeStruct((N, HD), BF),
        ],
        compiler_params=params(),
        cost_estimate=cost(8 * N * SRC * BIG * HD, 18 * 10**6),
        name="grads_a",
    )(dout, e, inv, qn, kt, vn)


def grads_b_body(rows, e_ref, inv_ref, qn_ref, kt_ref, vn_ref, dot_t, dot_n, dq_ref, out_ref, acc):
    i = pl.program_id(0)
    base = SRC * BIG

    @pl.when(i == 0)
    def _():
        acc[...] = dq_ref[...]

    k0 = pl.multiple_of(base + i * rows, 128)
    dv, dk = grads_block(k0, rows, e_ref, inv_ref, qn_ref, kt_ref, vn_ref, dot_t, dot_n, acc)
    for j in range(rows // SMALL):
        a = j * SMALL
        out_ref[i * (rows // SMALL) + j, 0:HD, :] = jnp.concatenate(
            [dv[:, a : a + SMALL], dk[:, a : a + SMALL]], axis=1
        )

    @pl.when(i == pl.num_programs(0) - 1)
    def _():
        for s in range(SRC):
            out_ref[s, HD : 2 * HD, :] = (acc[:, s * BIG : (s + 1) * BIG] * SCALE).astype(BF)
            a = base + s * SMALL
            b = acc[:, a : a + SMALL] * SCALE
            out_ref[s, 2 * HD : 2 * HD + HALF, :] = jnp.concatenate(
                [b[:HALF], b[HALF:]], axis=1
            ).astype(BF)


def grads_b(e, inv, qn, kt, vn, dot_t, dot_n, dq, rows=256):
    off = SRC * BIG // rows
    return pl.pallas_call(
        functools.partial(grads_b_body, rows),
        grid=(SRC * SMALL // rows,),
        in_specs=[
            pl.BlockSpec((rows, N), lambda i: (i + off, 0)),
            whole(8, N),
            whole(N, HD),
            whole(HD, N),
            whole(N, EXT),
            whole(EXT, N),
            whole(N, HD),
            whole(HD, N),
        ],
        out_specs=whole(SRC, 256, 128),
        out_shape=jax.ShapeDtypeStruct((SRC, 256, 128), BF),
        scratch_shapes=[pltpu.VMEM((HD, N), F32)],
        compiler_params=params(),
        cost_estimate=cost(8 * N * SRC * SMALL * HD, 11 * 10**6),
        name="grads_b",
    )(e, inv, qn, kt, vn, dot_t, dot_n, dq)


def unpack_body(a_ref, b_ref, dq_ref, dk_ref, dv_ref, dw_ref):
    def rows(ref, sl, lanes):
        return jnp.concatenate([ref[h, sl, lanes] for h in range(HEADS)], axis=0).T

    dv_ref[0, 0:BIG] = rows(a_ref, slice(0, HD), slice(0, BIG))
    dk_ref[0, 0:BIG] = rows(a_ref, slice(0, HD), slice(BIG, 2 * BIG))
    both = rows(b_ref, slice(0, HD), slice(0, BIG))
    dv_ref[0, BIG:TOK] = both[:SMALL]
    dk_ref[0, BIG:TOK] = both[SMALL:]
    dq_ref[0, 0:BIG] = rows(b_ref, slice(HD, 2 * HD), slice(0, BIG))
    tail = []
    for h in range(HEADS):
        t = b_ref[h, 2 * HD : 2 * HD + HALF, :].astype(F32)
        tail += [t[:, :SMALL], t[:, SMALL:]]
    dq_ref[0, BIG:TOK] = jnp.concatenate(tail, axis=0).T.astype(BF)
    for half in range(2):
        pieces = [b_ref[2 * g + half, 200:256, :].astype(F32) for g in range(8)]
        for c in range(2):
            for j in range(5):
                r = c * 25 + j * 5
                a = half * 640 + j * 128
                dw_ref[c * HALF : (c + 1) * HALF, a : a + 128] = jnp.concatenate(
                    [p[r : r + 5] for p in pieces], axis=0
                )


def unpack(a, b):
    shape = jax.ShapeDtypeStruct((1, TOK, D), BF)
    return pl.pallas_call(
        unpack_body,
        out_shape=[shape] * 3 + [jax.ShapeDtypeStruct((HD, D), F32)],
        compiler_params=params(),
        cost_estimate=cost(0, 3 * 10**6),
        name="unpack",
    )(a, b)


UP = [(i, (i + 1) % 8) for i in range(8)]
DOWN = [(i, (i - 1) % 8) for i in range(8)]


def body(query, keys, values, attn, d_block, w_out):
    c = lax.axis_index("c")
    yl = lax.axis_index("yl")
    z = lax.axis_index("z")
    swap = [(0, 1), (1, 0)]

    def exchange(x):
        return lax.all_to_all(x, SEQ, 0, 0, tiled=True)

    w_half = lax.dynamic_slice_in_dim(w_out, c * HALF, HALF, 0)
    pair = jnp.stack([w_half, lax.ppermute(w_half, "yl", swap)])
    query, keys, values, attn, d_block, pair = lax.optimization_barrier(
        (query, keys, values, attn, d_block, pair)
    )
    def scalar(i):
        return i.reshape(1).astype(jnp.int32)

    def up(block):
        return lax.ppermute(block, "z", UP)

    def down(block):
        return lax.ppermute(block, "z", DOWN)

    hold = lax.optimization_barrier
    g_oth = lax.ppermute(d_block, "c", swap)
    f1, g1, packed = hold((up(pair), down(pair), pack_qkv(query, keys, values)))
    qkv = exchange(packed)
    f2, g2, attn = hold((up(f1), down(g1), attn))
    a_own, a_send = split_attn(scalar(c), attn)
    f3, g3, a_oth, g_oth = hold((up(f2), down(g2), lax.ppermute(a_send, "c", swap), g_oth))
    keep, give, gx, ax = weight_share(scalar(yl), d_block, g_oth, a_own, a_oth)
    came = lax.ppermute(give, "yl", swap)
    blocks = [pair, f1, g1, f2, g2, f3, g3, up(f3)]

    zs = [(z + o) % 8 for o in OFFSETS]
    ids = jnp.stack([y * 8 + k for k in zs for y in (yl, 1 - yl)]).astype(jnp.int32)
    dout, qkv = lax.optimization_barrier((out_grad(ids, blocks, gx, ax), qkv))
    dout = exchange(dout)

    e, inv, qn, kt, vn = scores(qkv)
    both = (keep.astype(F32) + came.astype(F32)).astype(BF)
    both, e = lax.optimization_barrier((both, e))
    part = lax.all_to_all(both, "z", 0, 0, tiled=True)
    first, dq, dot_t, dot_n = grads_a(dout, e, inv, qn, kt, vn)
    first = exchange(lax.dynamic_update_slice(first, sum_z(part), (0, HD, 0)))
    second = grads_b(e, inv, qn, kt, vn, dot_t, dot_n, dq)
    second = exchange(lax.dynamic_update_slice(second, sum_seq(first[:, HD:]), (0, 200, 0)))
    d_query, d_keys, d_values, d_weight = unpack(first, second)
    return d_query, d_keys, d_values, d_weight


def solution(mesh):
    finer = Mesh(mesh.devices.reshape(2, 4, 2, 2, 8), ("yh", "x", "c", "yl", "z"))
    rows = P(DP, SEQ, None)
    weight = P(DP, None)
    return jax.shard_map(
        body,
        mesh=finer,
        in_specs=(rows,) * 5 + (weight,),
        out_specs=(rows,) * 3 + (weight,),
        check_vma=False,
    )
```

```python
import functools

import jax
import jax.numpy as jnp
from jax import lax
from jax.experimental import pallas as pl
from jax.experimental.pallas import tpu as pltpu
from jax.sharding import Mesh
from jax.sharding import PartitionSpec as P

BF = jnp.bfloat16
F32 = jnp.float32
HD = 80
HALF = 40
HEADS = 16
SRC = 16
N = 3072
TOK = 192
BIG = 128
SMALL = 64
EXT = 96
D = 1280
SCALE = HD**-0.5
LOG2E = 1.4426950408889634
VMEM_LIMIT = 56 * 1024 * 1024
SEQ = ("yh", "x", "c")
DP = ("yl", "z")
OFFSETS = (0, -1, 1, -2, 2, -3, 3, -4)


def params(limit=VMEM_LIMIT):
    return pltpu.CompilerParams(vmem_limit_bytes=limit)


def cost(flops, read, exps=0):
    return pl.CostEstimate(flops=flops, bytes_accessed=read, transcendentals=exps)


def whole(*shape):
    return pl.BlockSpec(shape, lambda *_: (0,) * len(shape))


def dot(a, b, ca, cb):
    return lax.dot_general(a, b, (((ca,), (cb,)), ((), ())), preferred_element_type=F32)


def lanes3(a, b):
    return jnp.concatenate([a[:, :BIG], b[:, :BIG], a[:, BIG:], b[:, BIG:]], axis=1)


def pack_qkv_body(q_ref, k_ref, v_ref, out_ref):
    qt, kt, vt = q_ref[0].T, k_ref[0].T, v_ref[0].T
    for h in range(HEADS):
        a = h * HD
        out_ref[h, 0:HD, :] = lanes3(qt[a : a + HD], kt[a : a + HD])
        v = vt[a : a + HD].astype(F32)
        out_ref[h, HD : HD + HALF, :] = lanes3(v[:HALF], v[HALF:]).astype(BF)


def pack_qkv(q, k, v):
    return pl.pallas_call(
        pack_qkv_body,
        out_shape=jax.ShapeDtypeStruct((HEADS, HD + HALF, 384), BF),
        compiler_params=params(),
        cost_estimate=cost(0, 3 * 10**6),
        name="pack_qkv",
    )(q, k, v)


def split_attn_body(c_ref, a_ref, own_ref, send_ref, at):
    at[...] = a_ref[0].T.astype(F32)
    c = c_ref[0]
    for h in range(HEADS):
        keep = pl.multiple_of(h * HD + c * HALF, 8)
        give = pl.multiple_of(h * HD + (1 - c) * HALF, 8)
        own_ref[h] = at[pl.ds(keep, HALF), :].astype(BF)
        send_ref[h] = at[pl.ds(give, HALF), :].astype(BF)


def split_attn(c, attn):
    vm = pl.BlockSpec(memory_space=pltpu.VMEM)
    shape = jax.ShapeDtypeStruct((HEADS, HALF, TOK), BF)
    return pl.pallas_call(
        split_attn_body,
        in_specs=[pl.BlockSpec(memory_space=pltpu.SMEM), vm],
        out_specs=[vm, vm],
        out_shape=[shape, shape],
        scratch_shapes=[pltpu.VMEM((D, TOK), F32)],
        compiler_params=params(),
        cost_estimate=cost(0, 10**6),
        name="split_attn",
    )(c, attn)


def weight_share_body(y_ref, g_own, g_oth, a_own, a_oth, keep_ref, give_ref, gx_ref, ax_ref, acc):
    gx_ref[0:128] = g_own[0, 0:128]
    gx_ref[128:256] = g_oth[0, 0:128]
    gx_ref[256:320] = g_own[0, 128:192]
    gx_ref[320:384] = g_oth[0, 128:192]
    for h in range(HEADS):
        ax_ref[h] = lanes3(a_own[h].astype(F32), a_oth[h].astype(F32)).astype(BF)
    rows = jnp.concatenate([ax_ref[h].astype(F32) for h in range(HEADS)], axis=0).astype(BF)
    acc[...] = dot(rows, gx_ref[...], 1, 0)
    y = y_ref[0]
    for k in range(8):
        keep = pl.multiple_of((y * 8 + k) * HALF, 8)
        give = pl.multiple_of(((1 - y) * 8 + k) * HALF, 8)
        keep_ref[k] = acc[pl.ds(keep, HALF), :].astype(BF)
        give_ref[k] = acc[pl.ds(give, HALF), :].astype(BF)


def weight_share(y, g_own, g_oth, a_own, a_oth):
    vm = pl.BlockSpec(memory_space=pltpu.VMEM)
    return pl.pallas_call(
        weight_share_body,
        in_specs=[pl.BlockSpec(memory_space=pltpu.SMEM)] + [vm] * 4,
        out_specs=[vm] * 4,
        out_shape=[
            jax.ShapeDtypeStruct((8, HALF, D), BF),
            jax.ShapeDtypeStruct((8, HALF, D), BF),
            jax.ShapeDtypeStruct((384, D), BF),
            jax.ShapeDtypeStruct((HEADS, HALF, 384), BF),
        ],
        scratch_shapes=[pltpu.VMEM((640, D), F32)],
        compiler_params=params(),
        cost_estimate=cost(2 * 640 * 384 * D, 6 * 10**6),
        name="weight_share",
    )(y, g_own, g_oth, a_own, a_oth)


def out_grad_body(ids, *refs):
    w_refs, (gx_ref, ax_ref, out_ref, w, acc) = refs[:8], refs[8:]
    for r in range(8):
        both = jnp.concatenate([w_refs[r][0].astype(F32), w_refs[r][1].astype(F32)], axis=0)
        w[r * HD : (r + 1) * HD] = both.astype(BF)
    acc[...] = dot(w[...], gx_ref[...], 1, 1)
    for r in range(HEADS):
        h = ids[r]
        low = acc[r * HALF : (r + 1) * HALF].astype(BF).astype(F32)
        minus = -jnp.sum(low * ax_ref[h].astype(F32), axis=0, keepdims=True)
        p1 = minus.astype(BF).astype(F32)
        p2 = (minus - p1).astype(BF).astype(F32)
        p3 = minus - p1 - p2
        pad = jnp.zeros((5, 384), F32)
        out_ref[h] = jnp.concatenate([low, p1, p2, p3, pad], axis=0).astype(BF)


def out_grad(ids, blocks, gx, ax):
    vm = pl.BlockSpec(memory_space=pltpu.VMEM)
    return pl.pallas_call(
        out_grad_body,
        in_specs=[pl.BlockSpec(memory_space=pltpu.SMEM)] + [vm] * 10,
        out_specs=vm,
        out_shape=jax.ShapeDtypeStruct((HEADS, 48, 384), BF),
        scratch_shapes=[pltpu.VMEM((640, D), BF), pltpu.VMEM((640, 384), F32)],
        compiler_params=params(),
        cost_estimate=cost(2 * 640 * 384 * D, 4 * 10**6),
        name="out_grad",
    )(ids, *blocks, gx, ax)


def each_place(put):
    for s in range(SRC):
        put(s * BIG, ((s, 0),))
    for s in range(0, SRC, 2):
        put(SRC * BIG + s * SMALL, ((s, 1), (s + 1, 1)))


def piece(x_ref, s, rows, col, small):
    if small:
        a = 2 * BIG + col * SMALL
        return x_ref[s, rows, a : a + SMALL]
    return x_ref[s, rows, col * BIG : (col + 1) * BIG]


def joined(parts):
    return parts[0] if len(parts) == 1 else jnp.concatenate(parts, axis=1)


def score_half(kn, q, s_new, s_old, m_old, emit, chunk, cols):
    m = jnp.full((8, cols), -jnp.inf, F32)
    total = jnp.zeros((8, cols), F32)
    for r in range(0, N, chunk):
        if q is not None:
            s = dot(kn[r : r + chunk, :], q, 1, 0)
            s_new[r : r + chunk, :] = s
            m = jnp.maximum(m, jnp.max(s.reshape(chunk // 8, 8, cols), axis=0))
        if s_old is not None:
            e = jnp.exp2((s_old[r : r + chunk, :] - m_old) * (SCALE * LOG2E))
            total = total + jnp.sum(e.reshape(chunk // 8, 8, cols), axis=0)
            emit(r, e.astype(BF))
    return jnp.max(m, axis=0, keepdims=True), jnp.sum(total, axis=0, keepdims=True)


def prepare_body(x_ref, qt_ref, kn_ref, qn_ref, kt_ref, vn_ref):
    ones = jnp.concatenate([jnp.ones((8, 128), F32), jnp.zeros((8, 128), F32)], axis=0)

    def put(a, pieces):
        q = joined([piece(x_ref, s, slice(0, HD), 0, small) for s, small in pieces])
        k = joined([piece(x_ref, s, slice(0, HD), 1, small) for s, small in pieces])
        qt_ref[:, a : a + 128] = q
        qn_ref[a : a + 128, :] = q.T
        kt_ref[:, a : a + 128] = k
        kn_ref[a : a + 128, :] = k.T
        rows = slice(HD, HD + HALF)
        low = joined([piece(x_ref, s, rows, 0, small).astype(F32) for s, small in pieces])
        high = joined([piece(x_ref, s, rows, 1, small).astype(F32) for s, small in pieces])
        v = jnp.concatenate([low, high, ones], axis=0)
        vn_ref[a : a + 128, :] = v.T.astype(BF)

    each_place(put)


def prepare(qkv):
    return pl.pallas_call(
        prepare_body,
        out_shape=[
            jax.ShapeDtypeStruct((HD, N), BF),
            jax.ShapeDtypeStruct((N, HD), BF),
            jax.ShapeDtypeStruct((N, HD), BF),
            jax.ShapeDtypeStruct((HD, N), BF),
            jax.ShapeDtypeStruct((N, EXT), BF),
        ],
        compiler_params=params(),
        cost_estimate=cost(0, 5 * 10**6),
        name="prepare",
    )(qkv)


def scores_body(cols, chunk, begin, end, qt, kn, e_ref, inv_ref, sa, sb, ma):
    i = pl.program_id(0)

    @pl.when(i == 0)
    def _():
        m, _ = score_half(kn, qt[:, begin : begin + cols], sa, None, None, None, chunk, cols)
        ma[...] = jnp.broadcast_to(m, ma.shape)

    def q_block(b):
        return qt[:, pl.ds(pl.multiple_of(begin + b * cols, cols), cols)]

    def emit0(r, v):
        e_ref[r : r + chunk, 0:cols] = v

    def emit1(r, v):
        e_ref[r : r + chunk, cols : 2 * cols] = v

    mb, l0 = score_half(kn, q_block(2 * i + 1), sb, sa, ma[0:1, :], emit0, chunk, cols)
    nxt = jnp.minimum(2 * i + 2, (end - begin) // cols - 1)
    mn, l1 = score_half(kn, q_block(nxt), sa, sb, mb, emit1, chunk, cols)
    ma[...] = jnp.broadcast_to(mn, ma.shape)
    inv_ref[...] = jnp.broadcast_to(1.0 / jnp.concatenate([l0, l1], axis=1), (8, 2 * cols))


def scores(qt, kn, begin, end, cols=256, chunk=128):
    size = end - begin
    return pl.pallas_call(
        functools.partial(scores_body, cols, chunk, begin, end),
        grid=(size // cols // 2,),
        in_specs=[whole(HD, N), whole(N, HD)],
        out_specs=[
            pl.BlockSpec((N, 2 * cols), lambda i: (0, i)),
            pl.BlockSpec((8, 2 * cols), lambda i: (0, i)),
        ],
        out_shape=[
            jax.ShapeDtypeStruct((N, size), BF),
            jax.ShapeDtypeStruct((8, size), F32),
        ],
        scratch_shapes=[
            pltpu.VMEM((N, cols), F32),
            pltpu.VMEM((N, cols), F32),
            pltpu.VMEM((8, cols), F32),
        ],
        compiler_params=params(),
        cost_estimate=cost(2 * N * size * HD, 6 * size * N // 3, N * size),
        name="scores",
    )(qt, kn)


CUT = 2048


def grads_block(k0, rows, e1, e2, inv1, inv2, qn, kt, vn, dot_t, dot_n, acc):
    v = vn[pl.ds(k0, rows), :]
    k = kt[:, pl.ds(k0, rows)]
    dv = dk = None
    for sl, e_ref, inv in ((slice(0, CUT), e1, inv1), (slice(CUT, N), e2, inv2)):
        e = e_ref[...]
        dp = dot(v, dot_t[:, sl], 1, 0)
        ds = (e.astype(F32) * dp * inv[0:1, :]).astype(BF)
        v_part = dot(e, dot_n[sl, :], 1, 0)
        k_part = dot(ds, qn[sl, :], 1, 0)
        dv = v_part if dv is None else dv + v_part
        dk = k_part if dk is None else dk + k_part
        acc[:, sl] += dot(k, ds, 1, 0)
    return dv.T.astype(BF), (dk * SCALE).T.astype(BF)


def grads_a_body(rows, x_ref, e1, e2, inv1, inv2, qn_ref, kt_ref, vn_ref, out_ref, dq_ref, dot_t, dot_n):
    i = pl.program_id(0)

    @pl.when(i == 0)
    def _():
        def side(s, small, sl):
            own = piece(x_ref, s, sl, 0, small).astype(F32)
            other = piece(x_ref, s ^ 1, sl, 1, small).astype(F32)
            return own, other

        def put(a, pieces):
            feats = []
            sums = []
            for s, small in pieces:
                own, other = side(s, small, slice(0, 48))
                first, second = (own, other) if s % 2 == 0 else (other, own)
                feats.append(jnp.concatenate([first[:HALF], second[:HALF]], axis=0))
                sums.append(own[HALF:] + jnp.concatenate([jnp.zeros((3, own.shape[1]), F32), other[HALF : HALF + 3], jnp.zeros((2, own.shape[1]), F32)], axis=0))
            f = joined(feats)
            t = joined(sums)
            dot_t[:, a : a + 128] = jnp.concatenate([f, t, jnp.zeros((8, 128), F32)], axis=0).astype(BF)
            inv = inv1[0:1, a : a + 128] if a < CUT else inv2[0:1, a - CUT : a - CUT + 128]
            dot_n[a : a + 128, :] = (f * inv).T.astype(BF)

        each_place(put)
        dq_ref[...] = jnp.zeros_like(dq_ref)

    k0 = pl.multiple_of(i * rows, 128)
    dv, dk = grads_block(
        k0, rows, e1, e2, inv1, inv2, qn_ref, kt_ref, vn_ref, dot_t, dot_n, dq_ref
    )
    for j in range(rows // BIG):
        out_ref[j, 0:HD, 0:BIG] = dv[:, j * BIG : (j + 1) * BIG]
        out_ref[j, 0:HD, BIG : 2 * BIG] = dk[:, j * BIG : (j + 1) * BIG]


def grads_a(dout, e1, e2, inv1, inv2, qn, kt, vn, rows=256):
    return pl.pallas_call(
        functools.partial(grads_a_body, rows),
        grid=(SRC * BIG // rows,),
        in_specs=[
            whole(SRC, 48, 384),
            pl.BlockSpec((rows, CUT), lambda i: (i, 0)),
            pl.BlockSpec((rows, N - CUT), lambda i: (i, 0)),
            whole(8, CUT),
            whole(8, N - CUT),
            whole(N, HD),
            whole(HD, N),
            whole(N, EXT),
        ],
        out_specs=[
            pl.BlockSpec((rows // BIG, HD, 2 * BIG), lambda i: (i, 0, 0)),
            whole(HD, N),
            whole(EXT, N),
            whole(N, HD),
        ],
        out_shape=[
            jax.ShapeDtypeStruct((SRC, HD, 2 * BIG), BF),
            jax.ShapeDtypeStruct((HD, N), F32),
            jax.ShapeDtypeStruct((EXT, N), BF),
            jax.ShapeDtypeStruct((N, HD), BF),
        ],
        compiler_params=params(),
        cost_estimate=cost(8 * N * SRC * BIG * HD, 18 * 10**6),
        name="grads_a",
    )(dout, e1, e2, inv1, inv2, qn, kt, vn)


def grads_b_body(rows, e1, e2, inv1, inv2, qn_ref, kt_ref, vn_ref, dot_t, dot_n, dq_ref, out_ref, acc):
    i = pl.program_id(0)
    base = SRC * BIG

    @pl.when(i == 0)
    def _():
        acc[...] = dq_ref[...]

    k0 = pl.multiple_of(base + i * rows, 128)
    dv, dk = grads_block(
        k0, rows, e1, e2, inv1, inv2, qn_ref, kt_ref, vn_ref, dot_t, dot_n, acc
    )
    for j in range(rows // SMALL):
        a = j * SMALL
        out_ref[i * (rows // SMALL) + j, 0:HD, :] = jnp.concatenate(
            [dv[:, a : a + SMALL], dk[:, a : a + SMALL]], axis=1
        )

    @pl.when(i == pl.num_programs(0) - 1)
    def _():
        for s in range(SRC):
            out_ref[s, HD : 2 * HD, :] = (acc[:, s * BIG : (s + 1) * BIG] * SCALE).astype(BF)
            a = base + s * SMALL
            b = acc[:, a : a + SMALL] * SCALE
            out_ref[s, 2 * HD : 2 * HD + HALF, :] = jnp.concatenate(
                [b[:HALF], b[HALF:]], axis=1
            ).astype(BF)


def grads_b(e1, e2, inv1, inv2, qn, kt, vn, dot_t, dot_n, dq, rows=256):
    off = SRC * BIG // rows
    return pl.pallas_call(
        functools.partial(grads_b_body, rows),
        grid=(SRC * SMALL // rows,),
        in_specs=[
            pl.BlockSpec((rows, CUT), lambda i: (i + off, 0)),
            pl.BlockSpec((rows, N - CUT), lambda i: (i + off, 0)),
            whole(8, CUT),
            whole(8, N - CUT),
            whole(N, HD),
            whole(HD, N),
            whole(N, EXT),
            whole(EXT, N),
            whole(N, HD),
            whole(HD, N),
        ],
        out_specs=whole(SRC, 200, 128),
        out_shape=jax.ShapeDtypeStruct((SRC, 200, 128), BF),
        scratch_shapes=[pltpu.VMEM((HD, N), F32)],
        compiler_params=params(),
        cost_estimate=cost(8 * N * SRC * SMALL * HD, 11 * 10**6),
        name="grads_b",
    )(e1, e2, inv1, inv2, qn, kt, vn, dot_t, dot_n, dq)


def patch_rows(ref, sl, lanes):
    return jnp.concatenate([ref[h, sl, lanes] for h in range(HEADS)], axis=0).T


def unpack_a_body(a_ref, dk_ref, dv_ref):
    dv_ref[0] = patch_rows(a_ref, slice(0, HD), slice(0, BIG))
    dk_ref[0] = patch_rows(a_ref, slice(0, HD), slice(BIG, 2 * BIG))


def unpack_a(a):
    shape = jax.ShapeDtypeStruct((1, TOK, D), BF)
    spec = pl.BlockSpec((1, BIG, D), lambda i: (0, 0, 0))
    return pl.pallas_call(
        unpack_a_body,
        grid=(1,),
        in_specs=[whole(HEADS, HD, 2 * BIG)],
        out_specs=[spec, spec],
        out_shape=[shape, shape],
        compiler_params=params(),
        cost_estimate=cost(0, 2 * 10**6),
        name="unpack_a",
    )(a)


def unpack_b_body(at_ref, b_ref, w_own, w_oth, dk_in, dv_in, dq_ref, dk_ref, dv_ref, dw_ref):
    both = patch_rows(b_ref, slice(0, HD), slice(0, BIG))
    dv_ref[0] = both[:SMALL]
    dk_ref[0] = both[SMALL:]
    dq_ref[0, 0:BIG] = patch_rows(b_ref, slice(HD, 2 * HD), slice(0, BIG))
    tail = []
    for h in range(HEADS):
        t = b_ref[h, 2 * HD : 2 * HD + HALF, :].astype(F32)
        tail += [t[:, :SMALL], t[:, SMALL:]]
    dq_ref[0, BIG:TOK] = jnp.concatenate(tail, axis=0).T.astype(BF)
    c = at_ref[0]
    factor = 1.0 / float(16 * N) ** 0.5
    for ref, row in ((w_own, c), (w_oth, 1 - c)):
        dw_ref[pl.ds(pl.multiple_of(row * HALF, 8), HALF), :] = ref[...] * factor


def unpack_b(at, b, parts, dk, dv):
    shape = jax.ShapeDtypeStruct((1, TOK, D), BF)
    spec = pl.BlockSpec((1, SMALL, D), lambda i: (0, 2, 0))
    hbm = pl.BlockSpec(memory_space=pl.ANY)
    return pl.pallas_call(
        unpack_b_body,
        grid=(1,),
        in_specs=[pl.BlockSpec(memory_space=pltpu.SMEM), whole(HEADS, 200, 128)]
        + [whole(HALF, D)] * 2
        + [hbm, hbm],
        out_specs=[whole(1, TOK, D), spec, spec, whole(HD, D)],
        out_shape=[shape] * 3 + [jax.ShapeDtypeStruct((HD, D), F32)],
        input_output_aliases={4: 1, 5: 2},
        compiler_params=params(),
        cost_estimate=cost(0, 3 * 10**6),
        name="unpack_b",
    )(at, b, *parts, dk, dv)


UP = [(i, (i + 1) % 8) for i in range(8)]
DOWN = [(i, (i - 1) % 8) for i in range(8)]


def body(query, keys, values, attn, d_block, w_out):
    c = lax.axis_index("c")
    yl = lax.axis_index("yl")
    z = lax.axis_index("z")
    swap = [(0, 1), (1, 0)]

    def exchange(x):
        return lax.all_to_all(x, SEQ, 0, 0, tiled=True)

    hold = lax.optimization_barrier

    def scalar(*i):
        return jnp.stack(i).astype(jnp.int32)

    def up(block):
        return lax.ppermute(block, "z", UP)

    def down(block):
        return lax.ppermute(block, "z", DOWN)

    w_half = lax.dynamic_slice_in_dim(w_out, c * HALF, HALF, 0)
    pair = jnp.stack([w_half, lax.ppermute(w_half, "yl", swap)])
    g_oth = lax.ppermute(d_block, "c", swap)
    packed = pack_qkv(query, keys, values)
    pair, packed, g_oth, attn = hold((pair, packed, g_oth, attn))
    qkv = exchange(packed)
    f1, g1, attn = hold((up(pair), down(pair), attn))
    a_own, a_send = split_attn(scalar(c), attn)
    f2, g2, a_send = hold((up(f1), down(g1), a_send))
    a_oth = lax.ppermute(a_send, "c", swap)
    f3, g3, a_oth = hold((up(f2), down(g2), a_oth))
    keep, give, gx, ax = weight_share(scalar(yl), d_block, g_oth, a_own, a_oth)
    f4, give = hold((up(f3), give))
    came = lax.ppermute(give, "yl", swap)

    zs = [(z + o) % 8 for o in OFFSETS]
    ids = scalar(*[y * 8 + k for k in zs for y in (yl, 1 - yl)])
    dout = out_grad(ids, [pair, f1, g1, f2, g2, f3, g3, f4], gx, ax)
    dout, qkv = hold((dout, qkv))
    dout = exchange(dout)

    qt, kn, qn, kt, vn = prepare(qkv)
    e1, inv1 = scores(qt, kn, 0, CUT)
    came, qt, inv1 = hold((came, qt, inv1))
    part = (keep.astype(F32) + came.astype(F32)).astype(BF)
    part, dout, qt = hold((part, dout, qt))
    part = lax.all_to_all(part, "z", 0, 0, tiled=True)
    e2, inv2 = scores(qt, kn, CUT, N)
    first, dq, dot_t, dot_n = grads_a(dout, e1, e2, inv1, inv2, qn, kt, vn)
    first, part = hold((first, part))
    first = exchange(first)
    second = grads_b(e1, e2, inv1, inv2, qn, kt, vn, dot_t, dot_n, dq)
    mine = jnp.sum(part.astype(F32), axis=0)
    t = mine
    for k in range(1, 4):
        t = t + lax.ppermute(mine, "x", [(i, (i + k) % 4) for i in range(4)])
    second, t = hold((second, t))
    second = exchange(second)
    u = t + lax.ppermute(t, "yh", swap)
    d_keys, d_values = unpack_a(first)
    return unpack_b(scalar(c), second, [u, lax.ppermute(u, "c", swap)], d_keys, d_values)


def solution(mesh):
    finer = Mesh(mesh.devices.reshape(2, 4, 2, 2, 8), ("yh", "x", "c", "yl", "z"))
    rows = P(DP, SEQ, None)
    weight = P(DP, None)
    return jax.shard_map(
        body,
        mesh=finer,
        in_specs=(rows,) * 5 + (weight,),
        out_specs=(rows,) * 3 + (weight,),
        check_vma=False,
    )
```

```python
import functools

import jax
import jax.numpy as jnp
from jax import lax
from jax.experimental import pallas as pl
from jax.experimental.pallas import tpu as pltpu
from jax.sharding import Mesh
from jax.sharding import PartitionSpec as P

BF = jnp.bfloat16
F32 = jnp.float32
HD = 80
HALF = 40
HEADS = 16
SRC = 16
N = 3072
TOK = 192
BIG = 128
SMALL = 64
EXT = 96
D = 1280
SCALE = HD**-0.5
LOG2E = 1.4426950408889634
VMEM_LIMIT = 28 * 1024 * 1024
SEQ = ("yh", "x", "c")
DP = ("yl", "z")
OFFSETS = (0, -1, 1, -2, 2, -3, 3, -4)


def params(limit=VMEM_LIMIT):
    return pltpu.CompilerParams(vmem_limit_bytes=limit)


def cost(flops, read, exps=0):
    return pl.CostEstimate(flops=flops, bytes_accessed=read, transcendentals=exps)


def whole(*shape):
    return pl.BlockSpec(shape, lambda *_: (0,) * len(shape))


def dot(a, b, ca, cb):
    return lax.dot_general(a, b, (((ca,), (cb,)), ((), ())), preferred_element_type=F32)


def lanes3(a, b):
    return jnp.concatenate([a[:, :BIG], b[:, :BIG], a[:, BIG:], b[:, BIG:]], axis=1)


def pack_qkv_body(q_ref, k_ref, v_ref, out_ref):
    qt, kt, vt = q_ref[0].T, k_ref[0].T, v_ref[0].T
    for h in range(HEADS):
        a = h * HD
        out_ref[h, 0:HD, :] = lanes3(qt[a : a + HD], kt[a : a + HD])
        v = vt[a : a + HD].astype(F32)
        out_ref[h, HD : HD + HALF, :] = lanes3(v[:HALF], v[HALF:]).astype(BF)


def pack_qkv(q, k, v):
    return pl.pallas_call(
        pack_qkv_body,
        out_shape=jax.ShapeDtypeStruct((HEADS, HD + HALF, 384), BF),
        compiler_params=params(),
        cost_estimate=cost(0, 3 * 10**6),
        name="pack_qkv",
    )(q, k, v)


def split_attn_body(c_ref, a_ref, own_ref, send_ref, at):
    at[...] = a_ref[0].T.astype(F32)
    c = c_ref[0]
    for h in range(HEADS):
        keep = pl.multiple_of(h * HD + c * HALF, 8)
        give = pl.multiple_of(h * HD + (1 - c) * HALF, 8)
        own_ref[h] = at[pl.ds(keep, HALF), :].astype(BF)
        send_ref[h] = at[pl.ds(give, HALF), :].astype(BF)


def split_attn(c, attn):
    vm = pl.BlockSpec(memory_space=pltpu.VMEM)
    shape = jax.ShapeDtypeStruct((HEADS, HALF, TOK), BF)
    return pl.pallas_call(
        split_attn_body,
        in_specs=[pl.BlockSpec(memory_space=pltpu.SMEM), vm],
        out_specs=[vm, vm],
        out_shape=[shape, shape],
        scratch_shapes=[pltpu.VMEM((D, TOK), F32)],
        compiler_params=params(),
        cost_estimate=cost(0, 10**6),
        name="split_attn",
    )(c, attn)


def weight_share_body(y_ref, g_own, g_oth, a_own, a_oth, keep_ref, give_ref, gx_ref, ax_ref, acc):
    gx_ref[0:128] = g_own[0, 0:128]
    gx_ref[128:256] = g_oth[0, 0:128]
    gx_ref[256:320] = g_own[0, 128:192]
    gx_ref[320:384] = g_oth[0, 128:192]
    for h in range(HEADS):
        ax_ref[h] = lanes3(a_own[h].astype(F32), a_oth[h].astype(F32)).astype(BF)
    rows = jnp.concatenate([ax_ref[h].astype(F32) for h in range(HEADS)], axis=0).astype(BF)
    acc[...] = dot(rows, gx_ref[...], 1, 0)
    y = y_ref[0]
    for k in range(8):
        keep = pl.multiple_of((y * 8 + k) * HALF, 8)
        give = pl.multiple_of(((1 - y) * 8 + k) * HALF, 8)
        keep_ref[k] = acc[pl.ds(keep, HALF), :].astype(BF)
        give_ref[k] = acc[pl.ds(give, HALF), :].astype(BF)


def weight_share(y, g_own, g_oth, a_own, a_oth):
    vm = pl.BlockSpec(memory_space=pltpu.VMEM)
    return pl.pallas_call(
        weight_share_body,
        in_specs=[pl.BlockSpec(memory_space=pltpu.SMEM)] + [vm] * 4,
        out_specs=[vm] * 4,
        out_shape=[
            jax.ShapeDtypeStruct((8, HALF, D), BF),
            jax.ShapeDtypeStruct((8, HALF, D), BF),
            jax.ShapeDtypeStruct((384, D), BF),
            jax.ShapeDtypeStruct((HEADS, HALF, 384), BF),
        ],
        scratch_shapes=[pltpu.VMEM((640, D), F32)],
        compiler_params=params(),
        cost_estimate=cost(2 * 640 * 384 * D, 6 * 10**6),
        name="weight_share",
    )(y, g_own, g_oth, a_own, a_oth)


def out_grad_body(ids, *refs):
    w_refs, (gx_ref, ax_ref, out_ref, w, acc) = refs[:8], refs[8:]
    for r in range(8):
        both = jnp.concatenate([w_refs[r][0].astype(F32), w_refs[r][1].astype(F32)], axis=0)
        w[r * HD : (r + 1) * HD] = both.astype(BF)
    acc[...] = dot(w[...], gx_ref[...], 1, 1)
    for r in range(HEADS):
        h = ids[r]
        low = acc[r * HALF : (r + 1) * HALF].astype(BF).astype(F32)
        minus = -jnp.sum(low * ax_ref[h].astype(F32), axis=0, keepdims=True)
        p1 = minus.astype(BF).astype(F32)
        p2 = (minus - p1).astype(BF).astype(F32)
        p3 = minus - p1 - p2
        pad = jnp.zeros((5, 384), F32)
        out_ref[h] = jnp.concatenate([low, p1, p2, p3, pad], axis=0).astype(BF)


def out_grad(ids, blocks, gx, ax):
    vm = pl.BlockSpec(memory_space=pltpu.VMEM)
    return pl.pallas_call(
        out_grad_body,
        in_specs=[pl.BlockSpec(memory_space=pltpu.SMEM)] + [vm] * 10,
        out_specs=vm,
        out_shape=jax.ShapeDtypeStruct((HEADS, 48, 384), BF),
        scratch_shapes=[pltpu.VMEM((640, D), BF), pltpu.VMEM((640, 384), F32)],
        compiler_params=params(),
        cost_estimate=cost(2 * 640 * 384 * D, 4 * 10**6),
        name="out_grad",
    )(ids, *blocks, gx, ax)


def each_place(put):
    for s in range(SRC):
        put(s * BIG, ((s, 0),))
    for s in range(0, SRC, 2):
        put(SRC * BIG + s * SMALL, ((s, 1), (s + 1, 1)))


def piece(x_ref, s, rows, col, small):
    if small:
        a = 2 * BIG + col * SMALL
        return x_ref[s, rows, a : a + SMALL]
    return x_ref[s, rows, col * BIG : (col + 1) * BIG]


def joined(parts):
    return parts[0] if len(parts) == 1 else jnp.concatenate(parts, axis=1)


def score_half(kn, q, s_new, s_old, m_old, emit, chunk, cols):
    m = jnp.full((8, cols), -jnp.inf, F32)
    total = jnp.zeros((8, cols), F32)
    for r in range(0, N, chunk):
        if q is not None:
            s = dot(kn[r : r + chunk, :], q, 1, 0)
            s_new[r : r + chunk, :] = s
            m = jnp.maximum(m, jnp.max(s.reshape(chunk // 8, 8, cols), axis=0))
        if s_old is not None:
            e = jnp.exp2((s_old[r : r + chunk, :] - m_old) * (SCALE * LOG2E))
            total = total + jnp.sum(e.reshape(chunk // 8, 8, cols), axis=0)
            emit(r, e.astype(BF))
    return jnp.max(m, axis=0, keepdims=True), jnp.sum(total, axis=0, keepdims=True)


def prepare_body(x_ref, qt_ref, kn_ref, kt_ref, vn_ref):
    ones = jnp.concatenate([jnp.ones((8, 128), F32), jnp.zeros((8, 128), F32)], axis=0)

    def put(a, pieces):
        q = joined([piece(x_ref, s, slice(0, HD), 0, small) for s, small in pieces])
        k = joined([piece(x_ref, s, slice(0, HD), 1, small) for s, small in pieces])
        qt_ref[:, a : a + 128] = q
        kt_ref[:, a : a + 128] = k
        kn_ref[a : a + 128, :] = k.T
        rows = slice(HD, HD + HALF)
        low = joined([piece(x_ref, s, rows, 0, small).astype(F32) for s, small in pieces])
        high = joined([piece(x_ref, s, rows, 1, small).astype(F32) for s, small in pieces])
        v = jnp.concatenate([low, high, ones], axis=0)
        vn_ref[a : a + 128, :] = v.T.astype(BF)

    each_place(put)


def prepare(qkv):
    return pl.pallas_call(
        prepare_body,
        out_shape=[
            jax.ShapeDtypeStruct((HD, N), BF),
            jax.ShapeDtypeStruct((N, HD), BF),
            jax.ShapeDtypeStruct((HD, N), BF),
            jax.ShapeDtypeStruct((N, EXT), BF),
        ],
        compiler_params=params(),
        cost_estimate=cost(0, 5 * 10**6),
        name="prepare",
    )(qkv)


def scores_body(cols, chunk, begin, end, qt, kn, e_ref, inv_ref, sa, sb, ma):
    i = pl.program_id(0)

    @pl.when(i == 0)
    def _():
        m, _ = score_half(kn, qt[:, begin : begin + cols], sa, None, None, None, chunk, cols)
        ma[...] = jnp.broadcast_to(m, ma.shape)

    def q_block(b):
        return qt[:, pl.ds(pl.multiple_of(begin + b * cols, cols), cols)]

    def emit0(r, v):
        e_ref[r : r + chunk, 0:cols] = v

    def emit1(r, v):
        e_ref[r : r + chunk, cols : 2 * cols] = v

    mb, l0 = score_half(kn, q_block(2 * i + 1), sb, sa, ma[0:1, :], emit0, chunk, cols)
    nxt = jnp.minimum(2 * i + 2, (end - begin) // cols - 1)
    mn, l1 = score_half(kn, q_block(nxt), sa, sb, mb, emit1, chunk, cols)
    ma[...] = jnp.broadcast_to(mn, ma.shape)
    inv_ref[...] = jnp.broadcast_to(1.0 / jnp.concatenate([l0, l1], axis=1), (8, 2 * cols))


def scores(qt, kn, begin, end, cols=256, chunk=128):
    size = end - begin
    return pl.pallas_call(
        functools.partial(scores_body, cols, chunk, begin, end),
        grid=(size // cols // 2,),
        in_specs=[whole(HD, N), whole(N, HD)],
        out_specs=[
            pl.BlockSpec((N, 2 * cols), lambda i: (0, i)),
            pl.BlockSpec((8, 2 * cols), lambda i: (0, i)),
        ],
        out_shape=[
            jax.ShapeDtypeStruct((N, size), BF),
            jax.ShapeDtypeStruct((8, size), F32),
        ],
        scratch_shapes=[
            pltpu.VMEM((N, cols), F32),
            pltpu.VMEM((N, cols), F32),
            pltpu.VMEM((8, cols), F32),
        ],
        compiler_params=params(),
        cost_estimate=cost(2 * N * size * HD, 6 * size * N // 3, N * size),
        name="scores",
    )(qt, kn)


CUT = 2048


def grads_block(k0, rows, e1, e2, inv1, inv2, qt, kt, vn, dot_t, dot_n, acc):
    v = vn[pl.ds(k0, rows), :]
    k = kt[:, pl.ds(k0, rows)]
    dv = dk = None
    for sl, e_ref, inv in ((slice(0, CUT), e1, inv1), (slice(CUT, N), e2, inv2)):
        e = e_ref[...]
        dp = dot(v, dot_t[:, sl], 1, 0)
        ds = (e.astype(F32) * dp * inv[0:1, :]).astype(BF)
        v_part = dot(e, dot_n[:, sl], 1, 1)
        k_part = dot(ds, qt[:, sl], 1, 1)
        dv = v_part if dv is None else dv + v_part
        dk = k_part if dk is None else dk + k_part
        acc[:, sl] += dot(k, ds, 1, 0)
    return dv.T.astype(BF), (dk * SCALE).T.astype(BF)


def grads_a_body(rows, x_ref, e1, e2, inv1, inv2, qt_ref, kt_ref, vn_ref, out_ref, dq_ref, dot_t, dot_n):
    i = pl.program_id(0)

    @pl.when(i == 0)
    def _():
        def side(s, small, sl):
            own = piece(x_ref, s, sl, 0, small).astype(F32)
            other = piece(x_ref, s ^ 1, sl, 1, small).astype(F32)
            return own, other

        def put(a, pieces):
            feats = []
            sums = []
            for s, small in pieces:
                own, other = side(s, small, slice(0, 48))
                first, second = (own, other) if s % 2 == 0 else (other, own)
                feats.append(jnp.concatenate([first[:HALF], second[:HALF]], axis=0))
                sums.append(own[HALF:] + jnp.concatenate([jnp.zeros((3, own.shape[1]), F32), other[HALF : HALF + 3], jnp.zeros((2, own.shape[1]), F32)], axis=0))
            f = joined(feats)
            t = joined(sums)
            dot_t[:, a : a + 128] = jnp.concatenate([f, t, jnp.zeros((8, 128), F32)], axis=0).astype(BF)
            inv = inv1[0:1, a : a + 128] if a < CUT else inv2[0:1, a - CUT : a - CUT + 128]
            dot_n[:, a : a + 128] = (f * inv).astype(BF)

        each_place(put)
        dq_ref[...] = jnp.zeros_like(dq_ref)

    k0 = pl.multiple_of(i * rows, 128)
    dv, dk = grads_block(
        k0, rows, e1, e2, inv1, inv2, qt_ref, kt_ref, vn_ref, dot_t, dot_n, dq_ref
    )
    for j in range(rows // BIG):
        out_ref[j, 0:HD, 0:BIG] = dv[:, j * BIG : (j + 1) * BIG]
        out_ref[j, 0:HD, BIG : 2 * BIG] = dk[:, j * BIG : (j + 1) * BIG]


def grads_a(dout, e1, e2, inv1, inv2, qt, kt, vn, rows=512):
    return pl.pallas_call(
        functools.partial(grads_a_body, rows),
        grid=(SRC * BIG // rows,),
        in_specs=[
            whole(SRC, 48, 384),
            pl.BlockSpec((rows, CUT), lambda i: (i, 0)),
            pl.BlockSpec((rows, N - CUT), lambda i: (i, 0)),
            whole(8, CUT),
            whole(8, N - CUT),
            whole(HD, N),
            whole(HD, N),
            whole(N, EXT),
        ],
        out_specs=[
            pl.BlockSpec((rows // BIG, HD, 2 * BIG), lambda i: (i, 0, 0)),
            whole(HD, N),
            whole(EXT, N),
            whole(HD, N),
        ],
        out_shape=[
            jax.ShapeDtypeStruct((SRC, HD, 2 * BIG), BF),
            jax.ShapeDtypeStruct((HD, N), F32),
            jax.ShapeDtypeStruct((EXT, N), BF),
            jax.ShapeDtypeStruct((HD, N), BF),
        ],
        compiler_params=params(),
        cost_estimate=cost(8 * N * SRC * BIG * HD, 18 * 10**6),
        name="grads_a",
    )(dout, e1, e2, inv1, inv2, qt, kt, vn)


def grads_b_body(rows, e1, e2, inv1, inv2, qt_ref, kt_ref, vn_ref, dot_t, dot_n, dq_ref, out_ref, acc):
    i = pl.program_id(0)
    base = SRC * BIG

    @pl.when(i == 0)
    def _():
        acc[...] = dq_ref[...]

    k0 = pl.multiple_of(base + i * rows, 128)
    dv, dk = grads_block(
        k0, rows, e1, e2, inv1, inv2, qt_ref, kt_ref, vn_ref, dot_t, dot_n, acc
    )
    for j in range(rows // SMALL):
        a = j * SMALL
        out_ref[i * (rows // SMALL) + j, 0:HD, :] = jnp.concatenate(
            [dv[:, a : a + SMALL], dk[:, a : a + SMALL]], axis=1
        )

    @pl.when(i == pl.num_programs(0) - 1)
    def _():
        for s in range(SRC):
            out_ref[s, HD : 2 * HD, :] = (acc[:, s * BIG : (s + 1) * BIG] * SCALE).astype(BF)
            a = base + s * SMALL
            b = acc[:, a : a + SMALL] * SCALE
            out_ref[s, 2 * HD : 2 * HD + HALF, :] = jnp.concatenate(
                [b[:HALF], b[HALF:]], axis=1
            ).astype(BF)


def grads_b(e1, e2, inv1, inv2, qt, kt, vn, dot_t, dot_n, dq, rows=512):
    off = SRC * BIG // rows
    return pl.pallas_call(
        functools.partial(grads_b_body, rows),
        grid=(SRC * SMALL // rows,),
        in_specs=[
            pl.BlockSpec((rows, CUT), lambda i: (i + off, 0)),
            pl.BlockSpec((rows, N - CUT), lambda i: (i + off, 0)),
            whole(8, CUT),
            whole(8, N - CUT),
            whole(HD, N),
            whole(HD, N),
            whole(N, EXT),
            whole(EXT, N),
            whole(HD, N),
            whole(HD, N),
        ],
        out_specs=whole(SRC, 200, 128),
        out_shape=jax.ShapeDtypeStruct((SRC, 200, 128), BF),
        scratch_shapes=[pltpu.VMEM((HD, N), F32)],
        compiler_params=params(),
        cost_estimate=cost(8 * N * SRC * SMALL * HD, 11 * 10**6),
        name="grads_b",
    )(e1, e2, inv1, inv2, qt, kt, vn, dot_t, dot_n, dq)


def patch_rows(ref, sl, lanes):
    return jnp.concatenate([ref[h, sl, lanes] for h in range(HEADS)], axis=0).T


def unpack_a_body(a_ref, dk_ref, dv_ref):
    dv_ref[0] = patch_rows(a_ref, slice(0, HD), slice(0, BIG))
    dk_ref[0] = patch_rows(a_ref, slice(0, HD), slice(BIG, 2 * BIG))


def unpack_a(a):
    shape = jax.ShapeDtypeStruct((1, TOK, D), BF)
    spec = pl.BlockSpec((1, BIG, D), lambda i: (0, 0, 0))
    return pl.pallas_call(
        unpack_a_body,
        grid=(1,),
        in_specs=[whole(HEADS, HD, 2 * BIG)],
        out_specs=[spec, spec],
        out_shape=[shape, shape],
        compiler_params=params(),
        cost_estimate=cost(0, 2 * 10**6),
        name="unpack_a",
    )(a)


def unpack_b_body(at_ref, b_ref, w_own, w_oth, dk_in, dv_in, dq_ref, dk_ref, dv_ref, dw_ref):
    both = patch_rows(b_ref, slice(0, HD), slice(0, BIG))
    dv_ref[0] = both[:SMALL]
    dk_ref[0] = both[SMALL:]
    dq_ref[0, 0:BIG] = patch_rows(b_ref, slice(HD, 2 * HD), slice(0, BIG))
    tail = []
    for h in range(HEADS):
        t = b_ref[h, 2 * HD : 2 * HD + HALF, :].astype(F32)
        tail += [t[:, :SMALL], t[:, SMALL:]]
    dq_ref[0, BIG:TOK] = jnp.concatenate(tail, axis=0).T.astype(BF)
    c = at_ref[0]
    factor = 1.0 / float(16 * N) ** 0.5
    for ref, row in ((w_own, c), (w_oth, 1 - c)):
        dw_ref[pl.ds(pl.multiple_of(row * HALF, 8), HALF), :] = ref[...] * factor


def unpack_b(at, b, parts, dk, dv):
    shape = jax.ShapeDtypeStruct((1, TOK, D), BF)
    spec = pl.BlockSpec((1, SMALL, D), lambda i: (0, 2, 0))
    hbm = pl.BlockSpec(memory_space=pl.ANY)
    return pl.pallas_call(
        unpack_b_body,
        grid=(1,),
        in_specs=[pl.BlockSpec(memory_space=pltpu.SMEM), whole(HEADS, 200, 128)]
        + [whole(HALF, D)] * 2
        + [hbm, hbm],
        out_specs=[whole(1, TOK, D), spec, spec, whole(HD, D)],
        out_shape=[shape] * 3 + [jax.ShapeDtypeStruct((HD, D), F32)],
        input_output_aliases={4: 1, 5: 2},
        compiler_params=params(),
        cost_estimate=cost(0, 3 * 10**6),
        name="unpack_b",
    )(at, b, *parts, dk, dv)


UP = [(i, (i + 1) % 8) for i in range(8)]
DOWN = [(i, (i - 1) % 8) for i in range(8)]


def body(query, keys, values, attn, d_block, w_out):
    c = lax.axis_index("c")
    yl = lax.axis_index("yl")
    z = lax.axis_index("z")
    swap = [(0, 1), (1, 0)]

    def exchange(x):
        return lax.all_to_all(x, SEQ, 0, 0, tiled=True)

    hold = lax.optimization_barrier

    def scalar(*i):
        return jnp.stack(i).astype(jnp.int32)

    def up(block):
        return lax.ppermute(block, "z", UP)

    def down(block):
        return lax.ppermute(block, "z", DOWN)

    w_half = lax.dynamic_slice_in_dim(w_out, c * HALF, HALF, 0)
    pair = jnp.stack([w_half, lax.ppermute(w_half, "yl", swap)])
    g_oth = lax.ppermute(d_block, "c", swap)
    packed = pack_qkv(query, keys, values)
    pair, packed, g_oth, attn = hold((pair, packed, g_oth, attn))
    qkv = exchange(packed)
    f1, g1, attn = hold((up(pair), down(pair), attn))
    a_own, a_send = split_attn(scalar(c), attn)
    f2, g2, a_send = hold((up(f1), down(g1), a_send))
    a_oth = lax.ppermute(a_send, "c", swap)
    f3, g3, a_oth = hold((up(f2), down(g2), a_oth))
    keep, give, gx, ax = weight_share(scalar(yl), d_block, g_oth, a_own, a_oth)
    f4, give = hold((up(f3), give))
    came = lax.ppermute(give, "yl", swap)

    zs = [(z + o) % 8 for o in OFFSETS]
    ids = scalar(*[y * 8 + k for k in zs for y in (yl, 1 - yl)])
    dout = out_grad(ids, [pair, f1, g1, f2, g2, f3, g3, f4], gx, ax)
    dout, qkv = hold((dout, qkv))
    dout = exchange(dout)

    qt, kn, kt, vn = prepare(qkv)
    e1, inv1 = scores(qt, kn, 0, CUT)
    came, qt, inv1 = hold((came, qt, inv1))
    part = (keep.astype(F32) + came.astype(F32)).astype(BF)
    part, dout, qt = hold((part, dout, qt))
    part = lax.all_to_all(part, "z", 0, 0, tiled=True)
    e2, inv2 = scores(qt, kn, CUT, N)
    first, dq, dot_t, dot_n = grads_a(dout, e1, e2, inv1, inv2, qt, kt, vn)
    first, part = hold((first, part))
    first = exchange(first)
    second = grads_b(e1, e2, inv1, inv2, qt, kt, vn, dot_t, dot_n, dq)
    mine = jnp.sum(part.astype(F32), axis=0)
    t = mine
    for k in range(1, 4):
        t = t + lax.ppermute(mine, "x", [(i, (i + k) % 4) for i in range(4)])
    second, t = hold((second, t))
    second = exchange(second)
    other = lax.ppermute(t, "yh", swap)
    other, d_keys, d_values = hold((other, *unpack_a(first)))
    u = t + other
    return unpack_b(scalar(c), second, [u, lax.ppermute(u, "c", swap)], d_keys, d_values)


def solution(mesh):
    finer = Mesh(mesh.devices.reshape(2, 4, 2, 2, 8), ("yh", "x", "c", "yl", "z"))
    rows = P(DP, SEQ, None)
    weight = P(DP, None)
    return jax.shard_map(
        body,
        mesh=finer,
        in_specs=(rows,) * 5 + (weight,),
        out_specs=(rows,) * 3 + (weight,),
        check_vma=False,
    )
```

```python
import functools

import jax
import jax.numpy as jnp
from jax import lax
from jax.experimental import pallas as pl
from jax.experimental.pallas import tpu as pltpu
from jax.sharding import Mesh
from jax.sharding import PartitionSpec as P

BF = jnp.bfloat16
F32 = jnp.float32
HD = 80
HALF = 40
HEADS = 16
SRC = 16
N = 3072
TOK = 192
BIG = 128
SMALL = 64
EXT = 96
D = 1280
SCALE = HD**-0.5
LOG2E = 1.4426950408889634
VMEM_LIMIT = 56 * 1024 * 1024
SEQ = ("yh", "x", "c")
DP = ("yl", "z")
OFFSETS = (0, -1, 1, -2, 2, -3, 3, -4)


def params(limit=VMEM_LIMIT):
    return pltpu.CompilerParams(vmem_limit_bytes=limit)


def cost(flops, read, exps=0):
    return pl.CostEstimate(flops=flops, bytes_accessed=read, transcendentals=exps)


def whole(*shape):
    return pl.BlockSpec(shape, lambda *_: (0,) * len(shape))


def dot(a, b, ca, cb):
    return lax.dot_general(a, b, (((ca,), (cb,)), ((), ())), preferred_element_type=F32)


def lanes3(a, b):
    return jnp.concatenate([a[:, :BIG], b[:, :BIG], a[:, BIG:], b[:, BIG:]], axis=1)


def pack_qkv_body(q_ref, k_ref, v_ref, out_ref):
    qt, kt, vt = q_ref[0].T, k_ref[0].T, v_ref[0].T
    for h in range(HEADS):
        a = h * HD
        out_ref[h, 0:HD, :] = lanes3(qt[a : a + HD], kt[a : a + HD])
        v = vt[a : a + HD].astype(F32)
        out_ref[h, HD : HD + HALF, :] = lanes3(v[:HALF], v[HALF:]).astype(BF)


def pack_qkv(q, k, v):
    return pl.pallas_call(
        pack_qkv_body,
        out_shape=jax.ShapeDtypeStruct((HEADS, HD + HALF, 384), BF),
        compiler_params=params(),
        cost_estimate=cost(0, 3 * 10**6),
        name="pack_qkv",
    )(q, k, v)


def split_attn_body(c_ref, a_ref, own_ref, send_ref, at):
    at[...] = a_ref[0].T.astype(F32)
    c = c_ref[0]
    for h in range(HEADS):
        keep = pl.multiple_of(h * HD + c * HALF, 8)
        give = pl.multiple_of(h * HD + (1 - c) * HALF, 8)
        own_ref[h] = at[pl.ds(keep, HALF), :].astype(BF)
        send_ref[h] = at[pl.ds(give, HALF), :].astype(BF)


def split_attn(c, attn):
    vm = pl.BlockSpec(memory_space=pltpu.VMEM)
    shape = jax.ShapeDtypeStruct((HEADS, HALF, TOK), BF)
    return pl.pallas_call(
        split_attn_body,
        in_specs=[pl.BlockSpec(memory_space=pltpu.SMEM), vm],
        out_specs=[vm, vm],
        out_shape=[shape, shape],
        scratch_shapes=[pltpu.VMEM((D, TOK), F32)],
        compiler_params=params(),
        cost_estimate=cost(0, 10**6),
        name="split_attn",
    )(c, attn)


def weight_share_body(y_ref, g_own, g_oth, a_own, a_oth, keep_ref, give_ref, gx_ref, ax_ref, acc):
    gx_ref[0:128] = g_own[0, 0:128]
    gx_ref[128:256] = g_oth[0, 0:128]
    gx_ref[256:320] = g_own[0, 128:192]
    gx_ref[320:384] = g_oth[0, 128:192]
    for h in range(HEADS):
        ax_ref[h] = lanes3(a_own[h].astype(F32), a_oth[h].astype(F32)).astype(BF)
    rows = jnp.concatenate([ax_ref[h].astype(F32) for h in range(HEADS)], axis=0).astype(BF)
    acc[...] = dot(rows, gx_ref[...], 1, 0)
    y = y_ref[0]
    for k in range(8):
        keep = pl.multiple_of((y * 8 + k) * HALF, 8)
        give = pl.multiple_of(((1 - y) * 8 + k) * HALF, 8)
        keep_ref[k] = acc[pl.ds(keep, HALF), :].astype(BF)
        give_ref[k] = acc[pl.ds(give, HALF), :].astype(BF)


def weight_share(y, g_own, g_oth, a_own, a_oth):
    vm = pl.BlockSpec(memory_space=pltpu.VMEM)
    return pl.pallas_call(
        weight_share_body,
        in_specs=[pl.BlockSpec(memory_space=pltpu.SMEM)] + [vm] * 4,
        out_specs=[vm] * 4,
        out_shape=[
            jax.ShapeDtypeStruct((8, HALF, D), BF),
            jax.ShapeDtypeStruct((8, HALF, D), BF),
            jax.ShapeDtypeStruct((384, D), BF),
            jax.ShapeDtypeStruct((HEADS, HALF, 384), BF),
        ],
        scratch_shapes=[pltpu.VMEM((640, D), F32)],
        compiler_params=params(),
        cost_estimate=cost(2 * 640 * 384 * D, 6 * 10**6),
        name="weight_share",
    )(y, g_own, g_oth, a_own, a_oth)


def out_grad_body(ids, *refs):
    w_refs, (gx_ref, ax_ref, out_ref, w, acc) = refs[:8], refs[8:]
    for r in range(8):
        both = jnp.concatenate([w_refs[r][0].astype(F32), w_refs[r][1].astype(F32)], axis=0)
        w[r * HD : (r + 1) * HD] = both.astype(BF)
    acc[...] = dot(w[...], gx_ref[...], 1, 1)
    for r in range(HEADS):
        h = ids[r]
        low = acc[r * HALF : (r + 1) * HALF].astype(BF).astype(F32)
        minus = -jnp.sum(low * ax_ref[h].astype(F32), axis=0, keepdims=True)
        p1 = minus.astype(BF).astype(F32)
        p2 = (minus - p1).astype(BF).astype(F32)
        p3 = minus - p1 - p2
        pad = jnp.zeros((5, 384), F32)
        out_ref[h] = jnp.concatenate([low, p1, p2, p3, pad], axis=0).astype(BF)


def out_grad(ids, blocks, gx, ax):
    vm = pl.BlockSpec(memory_space=pltpu.VMEM)
    return pl.pallas_call(
        out_grad_body,
        in_specs=[pl.BlockSpec(memory_space=pltpu.SMEM)] + [vm] * 10,
        out_specs=vm,
        out_shape=jax.ShapeDtypeStruct((HEADS, 48, 384), BF),
        scratch_shapes=[pltpu.VMEM((640, D), BF), pltpu.VMEM((640, 384), F32)],
        compiler_params=params(),
        cost_estimate=cost(2 * 640 * 384 * D, 4 * 10**6),
        name="out_grad",
    )(ids, *blocks, gx, ax)


def each_place(put):
    for s in range(SRC):
        put(s * BIG, ((s, 0),))
    for s in range(0, SRC, 2):
        put(SRC * BIG + s * SMALL, ((s, 1), (s + 1, 1)))


def piece(x_ref, s, rows, col, small):
    if small:
        a = 2 * BIG + col * SMALL
        return x_ref[s, rows, a : a + SMALL]
    return x_ref[s, rows, col * BIG : (col + 1) * BIG]


def joined(parts):
    return parts[0] if len(parts) == 1 else jnp.concatenate(parts, axis=1)


def score_half(kn, q, s_new, s_old, m_old, emit, chunk, cols):
    m = jnp.full((8, cols), -jnp.inf, F32)
    total = jnp.zeros((8, cols), F32)
    for r in range(0, N, chunk):
        if q is not None:
            s = dot(kn[r : r + chunk, :], q, 1, 0)
            s_new[r : r + chunk, :] = s
            m = jnp.maximum(m, jnp.max(s.reshape(chunk // 8, 8, cols), axis=0))
        if s_old is not None:
            e = jnp.exp2((s_old[r : r + chunk, :] - m_old) * (SCALE * LOG2E))
            total = total + jnp.sum(e.reshape(chunk // 8, 8, cols), axis=0)
            emit(r, e.astype(BF))
    return jnp.max(m, axis=0, keepdims=True), jnp.sum(total, axis=0, keepdims=True)


def prepare(x_ref, qt_ref, kn_ref, kt_ref, vn_ref):
    ones = jnp.concatenate([jnp.ones((8, 128), F32), jnp.zeros((8, 128), F32)], axis=0)

    def put(a, pieces):
        qt_ref[:, a : a + 128] = joined([piece(x_ref, s, slice(0, HD), 0, small) for s, small in pieces])
        k = joined([piece(x_ref, s, slice(0, HD), 1, small) for s, small in pieces])
        kt_ref[:, a : a + 128] = k
        kn_ref[a : a + 128, :] = k.T
        rows = slice(HD, HD + HALF)
        low = joined([piece(x_ref, s, rows, 0, small).astype(F32) for s, small in pieces])
        high = joined([piece(x_ref, s, rows, 1, small).astype(F32) for s, small in pieces])
        v = jnp.concatenate([low, high, ones], axis=0)
        vn_ref[a : a + 128, :] = v.T.astype(BF)

    each_place(put)


def scores_step(cols, chunk, begin, end, qt, kn, e_ref, inv_ref, sa, sb, ma):
    i = pl.program_id(0)

    @pl.when(i == 0)
    def _():
        m, _ = score_half(kn, qt[:, begin : begin + cols], sa, None, None, None, chunk, cols)
        ma[...] = jnp.broadcast_to(m, ma.shape)

    def q_block(b):
        return qt[:, pl.ds(pl.multiple_of(begin + b * cols, cols), cols)]

    def emit0(r, v):
        e_ref[r : r + chunk, 0:cols] = v

    def emit1(r, v):
        e_ref[r : r + chunk, cols : 2 * cols] = v

    mb, l0 = score_half(kn, q_block(2 * i + 1), sb, sa, ma[0:1, :], emit0, chunk, cols)
    nxt = jnp.minimum(2 * i + 2, (end - begin) // cols - 1)
    mn, l1 = score_half(kn, q_block(nxt), sa, sb, mb, emit1, chunk, cols)
    ma[...] = jnp.broadcast_to(mn, ma.shape)
    inv_ref[...] = jnp.broadcast_to(1.0 / jnp.concatenate([l0, l1], axis=1), (8, 2 * cols))


def scores_a_body(cols, chunk, x_ref, e_ref, inv_ref, qt, kn, kt_ref, vn_ref, sa, sb, ma):
    @pl.when(pl.program_id(0) == 0)
    def _():
        prepare(x_ref, qt, kn, kt_ref, vn_ref)

    scores_step(cols, chunk, 0, CUT, qt, kn, e_ref, inv_ref, sa, sb, ma)


def scores_b_body(cols, chunk, qt, kn, e_ref, inv_ref, sa, sb, ma):
    scores_step(cols, chunk, CUT, N, qt, kn, e_ref, inv_ref, sa, sb, ma)


def scores_call(body, name, size, more, operands, cols=256):
    return pl.pallas_call(
        body,
        grid=(size // cols // 2,),
        in_specs=[whole(*x.shape) for x in operands],
        out_specs=[
            pl.BlockSpec((N, 2 * cols), lambda i: (0, i)),
            pl.BlockSpec((8, 2 * cols), lambda i: (0, i)),
        ]
        + [whole(*shape) for shape in more],
        out_shape=[
            jax.ShapeDtypeStruct((N, size), BF),
            jax.ShapeDtypeStruct((8, size), F32),
        ]
        + [jax.ShapeDtypeStruct(shape, BF) for shape in more],
        scratch_shapes=[
            pltpu.VMEM((N, cols), F32),
            pltpu.VMEM((N, cols), F32),
            pltpu.VMEM((8, cols), F32),
        ],
        compiler_params=params(),
        cost_estimate=cost(2 * N * size * HD, 2 * size * N, N * size),
        name=name,
    )(*operands)


def scores_a(qkv):
    more = [(HD, N), (N, HD), (HD, N), (N, EXT)]
    return scores_call(functools.partial(scores_a_body, 256, 128), "scores_a", CUT, more, [qkv])


def scores_b(qt, kn):
    return scores_call(functools.partial(scores_b_body, 256, 128), "scores_b", N - CUT, [], [qt, kn])


CUT = 2048


def grads_block(k0, rows, e1, e2, inv1, inv2, qt, kt, vn, dot_t, dot_n, acc):
    v = vn[pl.ds(k0, rows), :]
    k = kt[:, pl.ds(k0, rows)]
    dv = dk = None
    for sl, e_ref, inv in ((slice(0, CUT), e1, inv1), (slice(CUT, N), e2, inv2)):
        e = e_ref[...]
        dp = dot(v, dot_t[:, sl], 1, 0)
        ds = (e.astype(F32) * dp * inv[0:1, :]).astype(BF)
        v_part = dot(e, dot_n[:, sl], 1, 1)
        k_part = dot(ds, qt[:, sl], 1, 1)
        dv = v_part if dv is None else dv + v_part
        dk = k_part if dk is None else dk + k_part
        acc[:, sl] += dot(k, ds, 1, 0)
    return dv.T.astype(BF), (dk * SCALE).T.astype(BF)


def grads_a_body(rows, x_ref, e1, e2, inv1, inv2, qt_ref, kt_ref, vn_ref, out_ref, dq_ref, dot_t, dot_n):
    i = pl.program_id(0)

    @pl.when(i == 0)
    def _():
        def side(s, small, sl):
            own = piece(x_ref, s, sl, 0, small).astype(F32)
            other = piece(x_ref, s ^ 1, sl, 1, small).astype(F32)
            return own, other

        def put(a, pieces):
            feats = []
            sums = []
            for s, small in pieces:
                own, other = side(s, small, slice(0, 48))
                first, second = (own, other) if s % 2 == 0 else (other, own)
                feats.append(jnp.concatenate([first[:HALF], second[:HALF]], axis=0))
                sums.append(own[HALF:] + jnp.concatenate([jnp.zeros((3, own.shape[1]), F32), other[HALF : HALF + 3], jnp.zeros((2, own.shape[1]), F32)], axis=0))
            f = joined(feats)
            t = joined(sums)
            dot_t[:, a : a + 128] = jnp.concatenate([f, t, jnp.zeros((8, 128), F32)], axis=0).astype(BF)
            inv = inv1[0:1, a : a + 128] if a < CUT else inv2[0:1, a - CUT : a - CUT + 128]
            dot_n[:, a : a + 128] = (f * inv).astype(BF)

        each_place(put)
        dq_ref[...] = jnp.zeros_like(dq_ref)

    k0 = pl.multiple_of(i * rows, 128)
    dv, dk = grads_block(
        k0, rows, e1, e2, inv1, inv2, qt_ref, kt_ref, vn_ref, dot_t, dot_n, dq_ref
    )
    for j in range(rows // BIG):
        out_ref[j, 0:HD, 0:BIG] = dv[:, j * BIG : (j + 1) * BIG]
        out_ref[j, 0:HD, BIG : 2 * BIG] = dk[:, j * BIG : (j + 1) * BIG]


def grads_a(dout, e1, e2, inv1, inv2, qt, kt, vn, rows=512):
    return pl.pallas_call(
        functools.partial(grads_a_body, rows),
        grid=(SRC * BIG // rows,),
        in_specs=[
            whole(SRC, 48, 384),
            pl.BlockSpec((rows, CUT), lambda i: (i, 0)),
            pl.BlockSpec((rows, N - CUT), lambda i: (i, 0)),
            whole(8, CUT),
            whole(8, N - CUT),
            whole(HD, N),
            whole(HD, N),
            whole(N, EXT),
        ],
        out_specs=[
            pl.BlockSpec((rows // BIG, HD, 2 * BIG), lambda i: (i, 0, 0)),
            whole(HD, N),
            whole(EXT, N),
            whole(HD, N),
        ],
        out_shape=[
            jax.ShapeDtypeStruct((SRC, HD, 2 * BIG), BF),
            jax.ShapeDtypeStruct((HD, N), F32),
            jax.ShapeDtypeStruct((EXT, N), BF),
            jax.ShapeDtypeStruct((HD, N), BF),
        ],
        compiler_params=params(),
        cost_estimate=cost(8 * N * SRC * BIG * HD, 18 * 10**6),
        name="grads_a",
    )(dout, e1, e2, inv1, inv2, qt, kt, vn)


def grads_b_body(rows, e1, e2, inv1, inv2, qt_ref, kt_ref, vn_ref, dot_t, dot_n, dq_ref, out_ref, acc):
    i = pl.program_id(0)
    base = SRC * BIG

    @pl.when(i == 0)
    def _():
        acc[...] = dq_ref[...]

    k0 = pl.multiple_of(base + i * rows, 128)
    dv, dk = grads_block(
        k0, rows, e1, e2, inv1, inv2, qt_ref, kt_ref, vn_ref, dot_t, dot_n, acc
    )
    for j in range(rows // SMALL):
        a = j * SMALL
        out_ref[i * (rows // SMALL) + j, 0:HD, :] = jnp.concatenate(
            [dv[:, a : a + SMALL], dk[:, a : a + SMALL]], axis=1
        )

    @pl.when(i == pl.num_programs(0) - 1)
    def _():
        for s in range(SRC):
            out_ref[s, HD : 2 * HD, :] = (acc[:, s * BIG : (s + 1) * BIG] * SCALE).astype(BF)
            a = base + s * SMALL
            b = acc[:, a : a + SMALL] * SCALE
            out_ref[s, 2 * HD : 2 * HD + HALF, :] = jnp.concatenate(
                [b[:HALF], b[HALF:]], axis=1
            ).astype(BF)


def grads_b(e1, e2, inv1, inv2, qt, kt, vn, dot_t, dot_n, dq, rows=512):
    off = SRC * BIG // rows
    return pl.pallas_call(
        functools.partial(grads_b_body, rows),
        grid=(SRC * SMALL // rows,),
        in_specs=[
            pl.BlockSpec((rows, CUT), lambda i: (i + off, 0)),
            pl.BlockSpec((rows, N - CUT), lambda i: (i + off, 0)),
            whole(8, CUT),
            whole(8, N - CUT),
            whole(HD, N),
            whole(HD, N),
            whole(N, EXT),
            whole(EXT, N),
            whole(HD, N),
            whole(HD, N),
        ],
        out_specs=whole(SRC, 200, 128),
        out_shape=jax.ShapeDtypeStruct((SRC, 200, 128), BF),
        scratch_shapes=[pltpu.VMEM((HD, N), F32)],
        compiler_params=params(),
        cost_estimate=cost(8 * N * SRC * SMALL * HD, 11 * 10**6),
        name="grads_b",
    )(e1, e2, inv1, inv2, qt, kt, vn, dot_t, dot_n, dq)


def patch_rows(ref, sl, lanes):
    return jnp.concatenate([ref[h, sl, lanes] for h in range(HEADS)], axis=0).T


def unpack_a_body(a_ref, dk_ref, dv_ref):
    dv_ref[0] = patch_rows(a_ref, slice(0, HD), slice(0, BIG))
    dk_ref[0] = patch_rows(a_ref, slice(0, HD), slice(BIG, 2 * BIG))


def unpack_a(a):
    shape = jax.ShapeDtypeStruct((1, TOK, D), BF)
    spec = pl.BlockSpec((1, BIG, D), lambda i: (0, 0, 0))
    return pl.pallas_call(
        unpack_a_body,
        grid=(1,),
        in_specs=[whole(HEADS, HD, 2 * BIG)],
        out_specs=[spec, spec],
        out_shape=[shape, shape],
        compiler_params=params(),
        cost_estimate=cost(0, 2 * 10**6),
        name="unpack_a",
    )(a)


def unpack_b_body(at_ref, b_ref, w_own, w_oth, dk_in, dv_in, dq_ref, dk_ref, dv_ref, dw_ref):
    both = patch_rows(b_ref, slice(0, HD), slice(0, BIG))
    dv_ref[0] = both[:SMALL]
    dk_ref[0] = both[SMALL:]
    dq_ref[0, 0:BIG] = patch_rows(b_ref, slice(HD, 2 * HD), slice(0, BIG))
    tail = []
    for h in range(HEADS):
        t = b_ref[h, 2 * HD : 2 * HD + HALF, :].astype(F32)
        tail += [t[:, :SMALL], t[:, SMALL:]]
    dq_ref[0, BIG:TOK] = jnp.concatenate(tail, axis=0).T.astype(BF)
    c = at_ref[0]
    factor = 1.0 / float(16 * N) ** 0.5
    for ref, row in ((w_own, c), (w_oth, 1 - c)):
        dw_ref[pl.ds(pl.multiple_of(row * HALF, 8), HALF), :] = ref[...] * factor


def unpack_b(at, b, parts, dk, dv):
    shape = jax.ShapeDtypeStruct((1, TOK, D), BF)
    spec = pl.BlockSpec((1, SMALL, D), lambda i: (0, 2, 0))
    hbm = pl.BlockSpec(memory_space=pl.ANY)
    return pl.pallas_call(
        unpack_b_body,
        grid=(1,),
        in_specs=[pl.BlockSpec(memory_space=pltpu.SMEM), whole(HEADS, 200, 128)]
        + [whole(HALF, D)] * 2
        + [hbm, hbm],
        out_specs=[whole(1, TOK, D), spec, spec, whole(HD, D)],
        out_shape=[shape] * 3 + [jax.ShapeDtypeStruct((HD, D), F32)],
        input_output_aliases={4: 1, 5: 2},
        compiler_params=params(),
        cost_estimate=cost(0, 3 * 10**6),
        name="unpack_b",
    )(at, b, *parts, dk, dv)


UP = [(i, (i + 1) % 8) for i in range(8)]
DOWN = [(i, (i - 1) % 8) for i in range(8)]


def body(query, keys, values, attn, d_block, w_out):
    c = lax.axis_index("c")
    yl = lax.axis_index("yl")
    z = lax.axis_index("z")
    swap = [(0, 1), (1, 0)]

    def exchange(x):
        return lax.all_to_all(x, SEQ, 0, 0, tiled=True)

    hold = lax.optimization_barrier

    def scalar(*i):
        return jnp.stack(i).astype(jnp.int32)

    def up(block):
        return lax.ppermute(block, "z", UP)

    def down(block):
        return lax.ppermute(block, "z", DOWN)

    w_half = lax.dynamic_slice_in_dim(w_out, c * HALF, HALF, 0)
    pair = jnp.stack([w_half, lax.ppermute(w_half, "yl", swap)])
    g_oth = lax.ppermute(d_block, "c", swap)
    packed = pack_qkv(query, keys, values)
    pair, packed, g_oth, attn = hold((pair, packed, g_oth, attn))
    qkv = exchange(packed)
    f1, g1, attn = hold((up(pair), down(pair), attn))
    a_own, a_send = split_attn(scalar(c), attn)
    f2, g2, a_send = hold((up(f1), down(g1), a_send))
    a_oth = lax.ppermute(a_send, "c", swap)
    f3, g3, a_oth = hold((up(f2), down(g2), a_oth))
    keep, give, gx, ax = weight_share(scalar(yl), d_block, g_oth, a_own, a_oth)
    f4, give = hold((up(f3), give))
    came = lax.ppermute(give, "yl", swap)

    zs = [(z + o) % 8 for o in OFFSETS]
    ids = scalar(*[y * 8 + k for k in zs for y in (yl, 1 - yl)])
    dout = out_grad(ids, [pair, f1, g1, f2, g2, f3, g3, f4], gx, ax)
    dout, qkv = hold((dout, qkv))
    dout = exchange(dout)

    e1, inv1, qt, kn, kt, vn = scores_a(qkv)
    came, qt, inv1 = hold((came, qt, inv1))
    part = (keep.astype(F32) + came.astype(F32)).astype(BF)
    part, dout, qt = hold((part, dout, qt))
    part = lax.all_to_all(part, "z", 0, 0, tiled=True)
    e2, inv2 = scores_b(qt, kn)
    first, dq, dot_t, dot_n = grads_a(dout, e1, e2, inv1, inv2, qt, kt, vn)
    first, part = hold((first, part))
    first = exchange(first)
    second = grads_b(e1, e2, inv1, inv2, qt, kt, vn, dot_t, dot_n, dq)
    mine = jnp.sum(part.astype(F32), axis=0)
    t = mine
    for k in range(1, 4):
        t = t + lax.ppermute(mine, "x", [(i, (i + k) % 4) for i in range(4)])
    second, t = hold((second, t))
    second = exchange(second)
    other = lax.ppermute(t, "yh", swap)
    other, d_keys, d_values = hold((other, *unpack_a(first)))
    u = t + other
    return unpack_b(scalar(c), second, [u, lax.ppermute(u, "c", swap)], d_keys, d_values)


def solution(mesh):
    finer = Mesh(mesh.devices.reshape(2, 4, 2, 2, 8), ("yh", "x", "c", "yl", "z"))
    rows = P(DP, SEQ, None)
    weight = P(DP, None)
    return jax.shard_map(
        body,
        mesh=finer,
        in_specs=(rows,) * 5 + (weight,),
        out_specs=(rows,) * 3 + (weight,),
        check_vma=False,
    )
```

```python
import functools

import jax
import jax.numpy as jnp
from jax import lax
from jax.experimental import pallas as pl
from jax.experimental.pallas import tpu as pltpu
from jax.sharding import Mesh
from jax.sharding import PartitionSpec as P

BF = jnp.bfloat16
F32 = jnp.float32
HD = 80
HALF = 40
HEADS = 16
SRC = 16
N = 3072
TOK = 192
BIG = 128
SMALL = 64
EXT = 96
D = 1280
SCALE = HD**-0.5
LOG2E = 1.4426950408889634
VMEM_LIMIT = 56 * 1024 * 1024
LESS = 28 * 1024 * 1024
SEQ = ("yh", "x", "c")
DP = ("yl", "z")
OFFSETS = (0, -1, 1, -2, 2, -3, 3, -4)


def params(limit=VMEM_LIMIT):
    return pltpu.CompilerParams(vmem_limit_bytes=limit)


def cost(flops, read, exps=0):
    return pl.CostEstimate(flops=flops, bytes_accessed=read, transcendentals=exps)


def whole(*shape):
    return pl.BlockSpec(shape, lambda *_: (0,) * len(shape))


def dot(a, b, ca, cb):
    return lax.dot_general(a, b, (((ca,), (cb,)), ((), ())), preferred_element_type=F32)


def lanes3(a, b):
    return jnp.concatenate([a[:, :BIG], b[:, :BIG], a[:, BIG:], b[:, BIG:]], axis=1)


def pack_qkv_body(q_ref, k_ref, v_ref, out_ref):
    qt, kt, vt = q_ref[0].T, k_ref[0].T, v_ref[0].T
    for h in range(HEADS):
        a = h * HD
        out_ref[h, 0:HD, :] = lanes3(qt[a : a + HD], kt[a : a + HD])
        v = vt[a : a + HD].astype(F32)
        out_ref[h, HD : HD + HALF, :] = lanes3(v[:HALF], v[HALF:]).astype(BF)


def pack_qkv(q, k, v):
    return pl.pallas_call(
        pack_qkv_body,
        out_shape=jax.ShapeDtypeStruct((HEADS, HD + HALF, 384), BF),
        compiler_params=params(),
        cost_estimate=cost(0, 3 * 10**6),
        name="pack_qkv",
    )(q, k, v)


def split_attn_body(c_ref, a_ref, own_ref, send_ref, at):
    at[...] = a_ref[0].T.astype(F32)
    c = c_ref[0]
    for h in range(HEADS):
        keep = pl.multiple_of(h * HD + c * HALF, 8)
        give = pl.multiple_of(h * HD + (1 - c) * HALF, 8)
        own_ref[h] = at[pl.ds(keep, HALF), :].astype(BF)
        send_ref[h] = at[pl.ds(give, HALF), :].astype(BF)


def split_attn(c, attn):
    vm = pl.BlockSpec(memory_space=pltpu.VMEM)
    shape = jax.ShapeDtypeStruct((HEADS, HALF, TOK), BF)
    return pl.pallas_call(
        split_attn_body,
        in_specs=[pl.BlockSpec(memory_space=pltpu.SMEM), vm],
        out_specs=[vm, vm],
        out_shape=[shape, shape],
        scratch_shapes=[pltpu.VMEM((D, TOK), F32)],
        compiler_params=params(),
        cost_estimate=cost(0, 10**6),
        name="split_attn",
    )(c, attn)


def weight_share_body(y_ref, g_own, g_oth, a_own, a_oth, keep_ref, give_ref, gx_ref, ax_ref, acc):
    gx_ref[0:128] = g_own[0, 0:128]
    gx_ref[128:256] = g_oth[0, 0:128]
    gx_ref[256:320] = g_own[0, 128:192]
    gx_ref[320:384] = g_oth[0, 128:192]
    for h in range(HEADS):
        ax_ref[h] = lanes3(a_own[h].astype(F32), a_oth[h].astype(F32)).astype(BF)
    rows = jnp.concatenate([ax_ref[h].astype(F32) for h in range(HEADS)], axis=0).astype(BF)
    acc[...] = dot(rows, gx_ref[...], 1, 0)
    y = y_ref[0]
    for k in range(8):
        keep = pl.multiple_of((y * 8 + k) * HALF, 8)
        give = pl.multiple_of(((1 - y) * 8 + k) * HALF, 8)
        keep_ref[k] = acc[pl.ds(keep, HALF), :].astype(BF)
        give_ref[k] = acc[pl.ds(give, HALF), :].astype(BF)


def weight_share(y, g_own, g_oth, a_own, a_oth):
    vm = pl.BlockSpec(memory_space=pltpu.VMEM)
    return pl.pallas_call(
        weight_share_body,
        in_specs=[pl.BlockSpec(memory_space=pltpu.SMEM)] + [vm] * 4,
        out_specs=[vm] * 4,
        out_shape=[
            jax.ShapeDtypeStruct((8, HALF, D), BF),
            jax.ShapeDtypeStruct((8, HALF, D), BF),
            jax.ShapeDtypeStruct((384, D), BF),
            jax.ShapeDtypeStruct((HEADS, HALF, 384), BF),
        ],
        scratch_shapes=[pltpu.VMEM((640, D), F32)],
        compiler_params=params(),
        cost_estimate=cost(2 * 640 * 384 * D, 6 * 10**6),
        name="weight_share",
    )(y, g_own, g_oth, a_own, a_oth)


def out_grad_body(ids, *refs):
    w_refs, (gx_ref, ax_ref, out_ref, w, acc) = refs[:8], refs[8:]
    for r in range(8):
        both = jnp.concatenate([w_refs[r][0].astype(F32), w_refs[r][1].astype(F32)], axis=0)
        w[r * HD : (r + 1) * HD] = both.astype(BF)
    acc[...] = dot(w[...], gx_ref[...], 1, 1)
    for r in range(HEADS):
        h = ids[r]
        low = acc[r * HALF : (r + 1) * HALF].astype(BF).astype(F32)
        minus = -jnp.sum(low * ax_ref[h].astype(F32), axis=0, keepdims=True)
        p1 = minus.astype(BF).astype(F32)
        p2 = (minus - p1).astype(BF).astype(F32)
        p3 = minus - p1 - p2
        pad = jnp.zeros((5, 384), F32)
        out_ref[h] = jnp.concatenate([low, p1, p2, p3, pad], axis=0).astype(BF)


def out_grad(ids, blocks, gx, ax):
    vm = pl.BlockSpec(memory_space=pltpu.VMEM)
    return pl.pallas_call(
        out_grad_body,
        in_specs=[pl.BlockSpec(memory_space=pltpu.SMEM)] + [vm] * 10,
        out_specs=vm,
        out_shape=jax.ShapeDtypeStruct((HEADS, 48, 384), BF),
        scratch_shapes=[pltpu.VMEM((640, D), BF), pltpu.VMEM((640, 384), F32)],
        compiler_params=params(),
        cost_estimate=cost(2 * 640 * 384 * D, 4 * 10**6),
        name="out_grad",
    )(ids, *blocks, gx, ax)


def each_place(put):
    for s in range(SRC):
        put(s * BIG, ((s, 0),))
    for s in range(0, SRC, 2):
        put(SRC * BIG + s * SMALL, ((s, 1), (s + 1, 1)))


def piece(x_ref, s, rows, col, small):
    if small:
        a = 2 * BIG + col * SMALL
        return x_ref[s, rows, a : a + SMALL]
    return x_ref[s, rows, col * BIG : (col + 1) * BIG]


def joined(parts):
    return parts[0] if len(parts) == 1 else jnp.concatenate(parts, axis=1)


def score_half(kn, q, s_new, s_old, m_old, emit, chunk, cols):
    m = jnp.full((8, cols), -jnp.inf, F32)
    total = jnp.zeros((8, cols), F32)
    for r in range(0, N, chunk):
        if q is not None:
            s = dot(kn[r : r + chunk, :], q, 1, 0)
            s_new[r : r + chunk, :] = s
            m = jnp.maximum(m, jnp.max(s.reshape(chunk // 8, 8, cols), axis=0))
        if s_old is not None:
            e = jnp.exp2((s_old[r : r + chunk, :] - m_old) * (SCALE * LOG2E))
            total = total + jnp.sum(e.reshape(chunk // 8, 8, cols), axis=0)
            emit(r, e.astype(BF))
    return jnp.max(m, axis=0, keepdims=True), jnp.sum(total, axis=0, keepdims=True)


def prepare(x_ref, qt_ref, kn_ref, kt_ref, vn_ref):
    ones = jnp.concatenate([jnp.ones((8, 128), F32), jnp.zeros((8, 128), F32)], axis=0)

    def put(a, pieces):
        qt_ref[:, a : a + 128] = joined([piece(x_ref, s, slice(0, HD), 0, small) for s, small in pieces])
        k = joined([piece(x_ref, s, slice(0, HD), 1, small) for s, small in pieces])
        kt_ref[:, a : a + 128] = k
        kn_ref[a : a + 128, :] = k.T
        rows = slice(HD, HD + HALF)
        low = joined([piece(x_ref, s, rows, 0, small).astype(F32) for s, small in pieces])
        high = joined([piece(x_ref, s, rows, 1, small).astype(F32) for s, small in pieces])
        v = jnp.concatenate([low, high, ones], axis=0)
        vn_ref[a : a + 128, :] = v.T.astype(BF)

    each_place(put)


def scores_step(cols, chunk, begin, end, qt, kn, e_ref, inv_ref, sa, sb, ma):
    i = pl.program_id(0)

    @pl.when(i == 0)
    def _():
        m, _ = score_half(kn, qt[:, begin : begin + cols], sa, None, None, None, chunk, cols)
        ma[...] = jnp.broadcast_to(m, ma.shape)

    def q_block(b):
        return qt[:, pl.ds(pl.multiple_of(begin + b * cols, cols), cols)]

    def emit0(r, v):
        e_ref[r : r + chunk, 0:cols] = v

    def emit1(r, v):
        e_ref[r : r + chunk, cols : 2 * cols] = v

    mb, l0 = score_half(kn, q_block(2 * i + 1), sb, sa, ma[0:1, :], emit0, chunk, cols)
    nxt = jnp.minimum(2 * i + 2, (end - begin) // cols - 1)
    mn, l1 = score_half(kn, q_block(nxt), sa, sb, mb, emit1, chunk, cols)
    ma[...] = jnp.broadcast_to(mn, ma.shape)
    inv_ref[...] = jnp.broadcast_to(1.0 / jnp.concatenate([l0, l1], axis=1), (8, 2 * cols))


def scores_a_body(cols, chunk, x_ref, e_ref, inv_ref, qt, kn, kt_ref, vn_ref, sa, sb, ma):
    @pl.when(pl.program_id(0) == 0)
    def _():
        prepare(x_ref, qt, kn, kt_ref, vn_ref)

    scores_step(cols, chunk, 0, CUT, qt, kn, e_ref, inv_ref, sa, sb, ma)


def scores_b_body(cols, chunk, qt, kn, e_ref, inv_ref, sa, sb, ma):
    scores_step(cols, chunk, CUT, N, qt, kn, e_ref, inv_ref, sa, sb, ma)


def scores_call(body, name, size, more, operands, cols=256):
    return pl.pallas_call(
        body,
        grid=(size // cols // 2,),
        in_specs=[whole(*x.shape) for x in operands],
        out_specs=[
            pl.BlockSpec((N, 2 * cols), lambda i: (0, i)),
            pl.BlockSpec((8, 2 * cols), lambda i: (0, i)),
        ]
        + [whole(*shape) for shape in more],
        out_shape=[
            jax.ShapeDtypeStruct((N, size), BF),
            jax.ShapeDtypeStruct((8, size), F32),
        ]
        + [jax.ShapeDtypeStruct(shape, BF) for shape in more],
        scratch_shapes=[
            pltpu.VMEM((N, cols), F32),
            pltpu.VMEM((N, cols), F32),
            pltpu.VMEM((8, cols), F32),
        ],
        compiler_params=params(),
        cost_estimate=cost(2 * N * size * HD, 2 * size * N, N * size),
        name=name,
    )(*operands)


def scores_a(qkv):
    more = [(HD, N), (N, HD), (HD, N), (N, EXT)]
    return scores_call(functools.partial(scores_a_body, 256, 128), "scores_a", CUT, more, [qkv])


def scores_b(qt, kn):
    return scores_call(functools.partial(scores_b_body, 256, 128), "scores_b", N - CUT, [], [qt, kn])


CUT = 2048


def grads_block(k0, rows, e1, e2, inv1, inv2, qt, kt, vn, dot_t, dot_n, acc):
    v = vn[pl.ds(k0, rows), :]
    k = kt[:, pl.ds(k0, rows)]
    dv = dk = None
    for sl, e_ref, inv in ((slice(0, CUT), e1, inv1), (slice(CUT, N), e2, inv2)):
        e = e_ref[...]
        dp = dot(v, dot_t[:, sl], 1, 0)
        ds = (e.astype(F32) * dp * inv[0:1, :]).astype(BF)
        v_part = dot(e, dot_n[:, sl], 1, 1)
        k_part = dot(ds, qt[:, sl], 1, 1)
        dv = v_part if dv is None else dv + v_part
        dk = k_part if dk is None else dk + k_part
        acc[:, sl] += dot(k, ds, 1, 0)
    return dv.T.astype(BF), (dk * SCALE).T.astype(BF)


def grads_a_body(rows, x_ref, e1, e2, inv1, inv2, qt_ref, kt_ref, vn_ref, out_ref, dq_ref, dot_t, dot_n):
    i = pl.program_id(0)

    @pl.when(i == 0)
    def _():
        def side(s, small, sl):
            own = piece(x_ref, s, sl, 0, small).astype(F32)
            other = piece(x_ref, s ^ 1, sl, 1, small).astype(F32)
            return own, other

        def put(a, pieces):
            feats = []
            sums = []
            for s, small in pieces:
                own, other = side(s, small, slice(0, 48))
                first, second = (own, other) if s % 2 == 0 else (other, own)
                feats.append(jnp.concatenate([first[:HALF], second[:HALF]], axis=0))
                sums.append(own[HALF:] + jnp.concatenate([jnp.zeros((3, own.shape[1]), F32), other[HALF : HALF + 3], jnp.zeros((2, own.shape[1]), F32)], axis=0))
            f = joined(feats)
            t = joined(sums)
            dot_t[:, a : a + 128] = jnp.concatenate([f, t, jnp.zeros((8, 128), F32)], axis=0).astype(BF)
            inv = inv1[0:1, a : a + 128] if a < CUT else inv2[0:1, a - CUT : a - CUT + 128]
            dot_n[:, a : a + 128] = (f * inv).astype(BF)

        each_place(put)
        dq_ref[...] = jnp.zeros_like(dq_ref)

    k0 = pl.multiple_of(i * rows, 128)
    dv, dk = grads_block(
        k0, rows, e1, e2, inv1, inv2, qt_ref, kt_ref, vn_ref, dot_t, dot_n, dq_ref
    )
    for j in range(rows // BIG):
        out_ref[j, 0:HD, 0:BIG] = dv[:, j * BIG : (j + 1) * BIG]
        out_ref[j, 0:HD, BIG : 2 * BIG] = dk[:, j * BIG : (j + 1) * BIG]


def grads_a(dout, e1, e2, inv1, inv2, qt, kt, vn, rows=512):
    return pl.pallas_call(
        functools.partial(grads_a_body, rows),
        grid=(SRC * BIG // rows,),
        in_specs=[
            whole(SRC, 48, 384),
            pl.BlockSpec((rows, CUT), lambda i: (i, 0)),
            pl.BlockSpec((rows, N - CUT), lambda i: (i, 0)),
            whole(8, CUT),
            whole(8, N - CUT),
            whole(HD, N),
            whole(HD, N),
            whole(N, EXT),
        ],
        out_specs=[
            pl.BlockSpec((rows // BIG, HD, 2 * BIG), lambda i: (i, 0, 0)),
            whole(HD, N),
            whole(EXT, N),
            whole(HD, N),
        ],
        out_shape=[
            jax.ShapeDtypeStruct((SRC, HD, 2 * BIG), BF),
            jax.ShapeDtypeStruct((HD, N), F32),
            jax.ShapeDtypeStruct((EXT, N), BF),
            jax.ShapeDtypeStruct((HD, N), BF),
        ],
        compiler_params=params(),
        cost_estimate=cost(8 * N * SRC * BIG * HD, 18 * 10**6),
        name="grads_a",
    )(dout, e1, e2, inv1, inv2, qt, kt, vn)


def grads_b_body(rows, e1, e2, inv1, inv2, qt_ref, kt_ref, vn_ref, dot_t, dot_n, dq_ref, out_ref, acc):
    i = pl.program_id(0)
    base = SRC * BIG

    @pl.when(i == 0)
    def _():
        acc[...] = dq_ref[...]

    k0 = pl.multiple_of(base + i * rows, 128)
    dv, dk = grads_block(
        k0, rows, e1, e2, inv1, inv2, qt_ref, kt_ref, vn_ref, dot_t, dot_n, acc
    )
    for j in range(rows // SMALL):
        a = j * SMALL
        out_ref[i * (rows // SMALL) + j, 0:HD, :] = jnp.concatenate(
            [dv[:, a : a + SMALL], dk[:, a : a + SMALL]], axis=1
        )

    @pl.when(i == pl.num_programs(0) - 1)
    def _():
        for s in range(SRC):
            out_ref[s, HD : 2 * HD, :] = (acc[:, s * BIG : (s + 1) * BIG] * SCALE).astype(BF)
            a = base + s * SMALL
            b = acc[:, a : a + SMALL] * SCALE
            out_ref[s, 2 * HD : 2 * HD + HALF, :] = jnp.concatenate(
                [b[:HALF], b[HALF:]], axis=1
            ).astype(BF)


def grads_b(e1, e2, inv1, inv2, qt, kt, vn, dot_t, dot_n, dq, rows=512):
    off = SRC * BIG // rows
    return pl.pallas_call(
        functools.partial(grads_b_body, rows),
        grid=(SRC * SMALL // rows,),
        in_specs=[
            pl.BlockSpec((rows, CUT), lambda i: (i + off, 0)),
            pl.BlockSpec((rows, N - CUT), lambda i: (i + off, 0)),
            whole(8, CUT),
            whole(8, N - CUT),
            whole(HD, N),
            whole(HD, N),
            whole(N, EXT),
            whole(EXT, N),
            whole(HD, N),
            whole(HD, N),
        ],
        out_specs=whole(SRC, 200, 128),
        out_shape=jax.ShapeDtypeStruct((SRC, 200, 128), BF),
        scratch_shapes=[pltpu.VMEM((HD, N), F32)],
        compiler_params=params(),
        cost_estimate=cost(8 * N * SRC * SMALL * HD, 11 * 10**6),
        name="grads_b",
    )(e1, e2, inv1, inv2, qt, kt, vn, dot_t, dot_n, dq)


def patch_rows(ref, sl, lanes):
    return jnp.concatenate([ref[h, sl, lanes] for h in range(HEADS)], axis=0).T


def unpack_a_body(a_ref, dk_ref, dv_ref):
    dv_ref[0] = patch_rows(a_ref, slice(0, HD), slice(0, BIG))
    dk_ref[0] = patch_rows(a_ref, slice(0, HD), slice(BIG, 2 * BIG))


def unpack_a(a):
    shape = jax.ShapeDtypeStruct((1, TOK, D), BF)
    spec = pl.BlockSpec((1, BIG, D), lambda i: (0, 0, 0))
    return pl.pallas_call(
        unpack_a_body,
        grid=(1,),
        in_specs=[whole(HEADS, HD, 2 * BIG)],
        out_specs=[spec, spec],
        out_shape=[shape, shape],
        compiler_params=params(LESS),
        cost_estimate=cost(0, 2 * 10**6),
        name="unpack_a",
    )(a)


def unpack_b_body(at_ref, b_ref, w0, w1, w2, w3, dk_in, dv_in, dq_ref, dk_ref, dv_ref, dw_ref):
    both = patch_rows(b_ref, slice(0, HD), slice(0, BIG))
    dv_ref[0] = both[:SMALL]
    dk_ref[0] = both[SMALL:]
    dq_ref[0, 0:BIG] = patch_rows(b_ref, slice(HD, 2 * HD), slice(0, BIG))
    tail = []
    for h in range(HEADS):
        t = b_ref[h, 2 * HD : 2 * HD + HALF, :].astype(F32)
        tail += [t[:, :SMALL], t[:, SMALL:]]
    dq_ref[0, BIG:TOK] = jnp.concatenate(tail, axis=0).T.astype(BF)
    c = at_ref[0]
    factor = 1.0 / float(16 * N) ** 0.5
    for ref, more, row in ((w0, w1, c), (w2, w3, 1 - c)):
        dw_ref[pl.ds(pl.multiple_of(row * HALF, 8), HALF), :] = (ref[...] + more[...]) * factor


def unpack_b(at, b, parts, dk, dv):
    shape = jax.ShapeDtypeStruct((1, TOK, D), BF)
    spec = pl.BlockSpec((1, SMALL, D), lambda i: (0, 2, 0))
    hbm = pl.BlockSpec(memory_space=pl.ANY)
    return pl.pallas_call(
        unpack_b_body,
        grid=(1,),
        in_specs=[pl.BlockSpec(memory_space=pltpu.SMEM), whole(HEADS, 200, 128)]
        + [whole(HALF, D)] * 4
        + [hbm, hbm],
        out_specs=[whole(1, TOK, D), spec, spec, whole(HD, D)],
        out_shape=[shape] * 3 + [jax.ShapeDtypeStruct((HD, D), F32)],
        input_output_aliases={6: 1, 7: 2},
        compiler_params=params(LESS),
        cost_estimate=cost(0, 3 * 10**6),
        name="unpack_b",
    )(at, b, *parts, dk, dv)


UP = [(i, (i + 1) % 8) for i in range(8)]
DOWN = [(i, (i - 1) % 8) for i in range(8)]


def body(query, keys, values, attn, d_block, w_out):
    c = lax.axis_index("c")
    yl = lax.axis_index("yl")
    z = lax.axis_index("z")
    swap = [(0, 1), (1, 0)]

    def exchange(x):
        return lax.all_to_all(x, SEQ, 0, 0, tiled=True)

    hold = lax.optimization_barrier

    def scalar(*i):
        return jnp.stack(i).astype(jnp.int32)

    def up(block):
        return lax.ppermute(block, "z", UP)

    def down(block):
        return lax.ppermute(block, "z", DOWN)

    w_half = lax.dynamic_slice_in_dim(w_out, c * HALF, HALF, 0)
    pair = jnp.stack([w_half, lax.ppermute(w_half, "yl", swap)])
    g_oth = lax.ppermute(d_block, "c", swap)
    packed = pack_qkv(query, keys, values)
    zs = [(z + o) % 8 for o in OFFSETS]
    ids = scalar(*[y * 8 + k for k in zs for y in (yl, 1 - yl)])
    pair, packed, g_oth, attn, ids = hold((pair, packed, g_oth, attn, ids))
    qkv = exchange(packed)
    f1, g1, attn = hold((up(pair), down(pair), attn))
    a_own, a_send = split_attn(scalar(c), attn)
    f2, g2, a_send = hold((up(f1), down(g1), a_send))
    a_oth = lax.ppermute(a_send, "c", swap)
    f3, g3, a_oth = hold((up(f2), down(g2), a_oth))
    keep, give, gx, ax = weight_share(scalar(yl), d_block, g_oth, a_own, a_oth)
    f4, give = hold((up(f3), give))
    came = lax.ppermute(give, "yl", swap)

    dout = out_grad(ids, [pair, f1, g1, f2, g2, f3, g3, f4], gx, ax)
    dout, qkv = hold((dout, qkv))
    dout = exchange(dout)

    e1, inv1, qt, kn, kt, vn = scores_a(qkv)
    came, qt, inv1 = hold((came, qt, inv1))
    part = (keep.astype(F32) + came.astype(F32)).astype(BF)
    part, dout, qt = hold((part, dout, qt))
    part = lax.all_to_all(part, "z", 0, 0, tiled=True)
    e2, inv2 = scores_b(qt, kn)
    first, dq, dot_t, dot_n = grads_a(dout, e1, e2, inv1, inv2, qt, kt, vn)
    first, part = hold((first, part))
    first = exchange(first)
    second = grads_b(e1, e2, inv1, inv2, qt, kt, vn, dot_t, dot_n, dq)
    mine = jnp.sum(part.astype(F32), axis=0)
    t = mine
    for k in range(1, 4):
        t = t + lax.ppermute(mine, "x", [(i, (i + k) % 4) for i in range(4)])
    second, t = hold((second, t))
    second = exchange(second)
    across = [(0, 3), (1, 2), (2, 1), (3, 0)]
    came_y = lax.ppermute(t, "yh", swap)
    came_c = lax.ppermute(t, "c", swap)
    came_yc = lax.ppermute(t, ("yh", "c"), across)
    d_keys, d_values = unpack_a(first)
    came_y, came_c, came_yc, d_keys, d_values = hold((came_y, came_c, came_yc, d_keys, d_values))
    return unpack_b(scalar(c), second, [t, came_y, came_c, came_yc], d_keys, d_values)


def solution(mesh):
    finer = Mesh(mesh.devices.reshape(2, 4, 2, 2, 8), ("yh", "x", "c", "yl", "z"))
    rows = P(DP, SEQ, None)
    weight = P(DP, None)
    return jax.shard_map(
        body,
        mesh=finer,
        in_specs=(rows,) * 5 + (weight,),
        out_specs=(rows,) * 3 + (weight,),
        check_vma=False,
    )
```

```python
import functools

import jax
import jax.numpy as jnp
from jax import lax
from jax.experimental import pallas as pl
from jax.experimental.pallas import tpu as pltpu
from jax.sharding import Mesh
from jax.sharding import PartitionSpec as P

BF = jnp.bfloat16
F32 = jnp.float32
HD = 80
HALF = 40
HEADS = 16
SRC = 16
N = 3072
TOK = 192
BIG = 128
SMALL = 64
EXT = 96
D = 1280
SCALE = HD**-0.5
LOG2E = 1.4426950408889634
VMEM_LIMIT = 56 * 1024 * 1024
LESS = 28 * 1024 * 1024
SEQ = ("yh", "x", "c")
DP = ("yl", "z")
OFFSETS = (0, -1, 1, -2, 2, -3, 3, -4)


def params(limit=VMEM_LIMIT):
    return pltpu.CompilerParams(vmem_limit_bytes=limit)


def cost(flops, read, exps=0):
    return pl.CostEstimate(flops=flops, bytes_accessed=read, transcendentals=exps)


def whole(*shape):
    return pl.BlockSpec(shape, lambda *_: (0,) * len(shape))


def dot(a, b, ca, cb):
    return lax.dot_general(a, b, (((ca,), (cb,)), ((), ())), preferred_element_type=F32)


def lanes3(a, b):
    return jnp.concatenate([a[:, :BIG], b[:, :BIG], a[:, BIG:], b[:, BIG:]], axis=1)


def pack_qkv_body(q_ref, k_ref, v_ref, out_ref):
    qt, kt, vt = q_ref[0].T, k_ref[0].T, v_ref[0].T
    for h in range(HEADS):
        a = h * HD
        out_ref[h, 0:HD, :] = lanes3(qt[a : a + HD], kt[a : a + HD])
        v = vt[a : a + HD].astype(F32)
        out_ref[h, HD : HD + HALF, :] = lanes3(v[:HALF], v[HALF:]).astype(BF)


def pack_qkv(q, k, v):
    return pl.pallas_call(
        pack_qkv_body,
        out_shape=jax.ShapeDtypeStruct((HEADS, HD + HALF, 384), BF),
        compiler_params=params(),
        cost_estimate=cost(0, 3 * 10**6),
        name="pack_qkv",
    )(q, k, v)


def split_attn_body(c_ref, a_ref, own_ref, send_ref, at):
    at[...] = a_ref[0].T.astype(F32)
    c = c_ref[0]
    for h in range(HEADS):
        keep = pl.multiple_of(h * HD + c * HALF, 8)
        give = pl.multiple_of(h * HD + (1 - c) * HALF, 8)
        own_ref[h] = at[pl.ds(keep, HALF), :].astype(BF)
        send_ref[h] = at[pl.ds(give, HALF), :].astype(BF)


def split_attn(c, attn):
    vm = pl.BlockSpec(memory_space=pltpu.VMEM)
    shape = jax.ShapeDtypeStruct((HEADS, HALF, TOK), BF)
    return pl.pallas_call(
        split_attn_body,
        in_specs=[pl.BlockSpec(memory_space=pltpu.SMEM), vm],
        out_specs=[vm, vm],
        out_shape=[shape, shape],
        scratch_shapes=[pltpu.VMEM((D, TOK), F32)],
        compiler_params=params(),
        cost_estimate=cost(0, 10**6),
        name="split_attn",
    )(c, attn)


def weight_share_body(y_ref, g_own, g_oth, a_own, a_oth, keep_ref, give_ref, gx_ref, ax_ref, acc):
    gx_ref[0:128] = g_own[0, 0:128]
    gx_ref[128:256] = g_oth[0, 0:128]
    gx_ref[256:320] = g_own[0, 128:192]
    gx_ref[320:384] = g_oth[0, 128:192]
    for h in range(HEADS):
        ax_ref[h] = lanes3(a_own[h].astype(F32), a_oth[h].astype(F32)).astype(BF)
    rows = jnp.concatenate([ax_ref[h].astype(F32) for h in range(HEADS)], axis=0).astype(BF)
    acc[...] = dot(rows, gx_ref[...], 1, 0)
    y = y_ref[0]
    for k in range(8):
        keep = pl.multiple_of((y * 8 + k) * HALF, 8)
        give = pl.multiple_of(((1 - y) * 8 + k) * HALF, 8)
        keep_ref[k] = acc[pl.ds(keep, HALF), :].astype(BF)
        give_ref[k] = acc[pl.ds(give, HALF), :].astype(BF)


def weight_share(y, g_own, g_oth, a_own, a_oth):
    vm = pl.BlockSpec(memory_space=pltpu.VMEM)
    return pl.pallas_call(
        weight_share_body,
        in_specs=[pl.BlockSpec(memory_space=pltpu.SMEM)] + [vm] * 4,
        out_specs=[vm] * 4,
        out_shape=[
            jax.ShapeDtypeStruct((8, HALF, D), BF),
            jax.ShapeDtypeStruct((8, HALF, D), BF),
            jax.ShapeDtypeStruct((384, D), BF),
            jax.ShapeDtypeStruct((HEADS, HALF, 384), BF),
        ],
        scratch_shapes=[pltpu.VMEM((640, D), F32)],
        compiler_params=params(),
        cost_estimate=cost(2 * 640 * 384 * D, 6 * 10**6),
        name="weight_share",
    )(y, g_own, g_oth, a_own, a_oth)


def out_grad_body(ids, *refs):
    w_refs, (gx_ref, ax_ref, out_ref, w, acc) = refs[:8], refs[8:]
    for r in range(8):
        both = jnp.concatenate([w_refs[r][0].astype(F32), w_refs[r][1].astype(F32)], axis=0)
        w[r * HD : (r + 1) * HD] = both.astype(BF)
    acc[...] = dot(w[...], gx_ref[...], 1, 1)
    for r in range(HEADS):
        h = ids[r]
        low = acc[r * HALF : (r + 1) * HALF].astype(BF).astype(F32)
        minus = -jnp.sum(low * ax_ref[h].astype(F32), axis=0, keepdims=True)
        p1 = minus.astype(BF).astype(F32)
        p2 = (minus - p1).astype(BF).astype(F32)
        p3 = minus - p1 - p2
        pad = jnp.zeros((5, 384), F32)
        out_ref[h] = jnp.concatenate([low, p1, p2, p3, pad], axis=0).astype(BF)


def out_grad(ids, blocks, gx, ax):
    vm = pl.BlockSpec(memory_space=pltpu.VMEM)
    return pl.pallas_call(
        out_grad_body,
        in_specs=[pl.BlockSpec(memory_space=pltpu.SMEM)] + [vm] * 10,
        out_specs=vm,
        out_shape=jax.ShapeDtypeStruct((HEADS, 48, 384), BF),
        scratch_shapes=[pltpu.VMEM((640, D), BF), pltpu.VMEM((640, 384), F32)],
        compiler_params=params(),
        cost_estimate=cost(2 * 640 * 384 * D, 4 * 10**6),
        name="out_grad",
    )(ids, *blocks, gx, ax)


def each_place(put):
    for s in range(SRC):
        put(s * BIG, ((s, 0),))
    for s in range(0, SRC, 2):
        put(SRC * BIG + s * SMALL, ((s, 1), (s + 1, 1)))


def piece(x_ref, s, rows, col, small):
    if small:
        a = 2 * BIG + col * SMALL
        return x_ref[s, rows, a : a + SMALL]
    return x_ref[s, rows, col * BIG : (col + 1) * BIG]


def joined(parts):
    return parts[0] if len(parts) == 1 else jnp.concatenate(parts, axis=1)


def score_half(kn, q, s_new, s_old, m_old, emit, chunk, cols):
    m = jnp.full((8, cols), -jnp.inf, F32)
    total = jnp.zeros((8, cols), F32)
    for r in range(0, N, chunk):
        if q is not None:
            s = dot(kn[r : r + chunk, :], q, 1, 0)
            s_new[r : r + chunk, :] = s
            m = jnp.maximum(m, jnp.max(s.reshape(chunk // 8, 8, cols), axis=0))
        if s_old is not None:
            e = jnp.exp2((s_old[r : r + chunk, :] - m_old) * (SCALE * LOG2E))
            total = total + jnp.sum(e.reshape(chunk // 8, 8, cols), axis=0)
            emit(r, e.astype(BF))
    return jnp.max(m, axis=0, keepdims=True), jnp.sum(total, axis=0, keepdims=True)


def prepare(x_ref, qt_ref, kn_ref, kt_ref, vn_ref):
    ones = jnp.concatenate([jnp.ones((8, 128), F32), jnp.zeros((8, 128), F32)], axis=0)

    def put(a, pieces):
        qt_ref[:, a : a + 128] = joined([piece(x_ref, s, slice(0, HD), 0, small) for s, small in pieces])
        k = joined([piece(x_ref, s, slice(0, HD), 1, small) for s, small in pieces])
        kt_ref[:, a : a + 128] = k
        kn_ref[a : a + 128, :] = k.T
        rows = slice(HD, HD + HALF)
        low = joined([piece(x_ref, s, rows, 0, small).astype(F32) for s, small in pieces])
        high = joined([piece(x_ref, s, rows, 1, small).astype(F32) for s, small in pieces])
        v = jnp.concatenate([low, high, ones], axis=0)
        vn_ref[a : a + 128, :] = v.T.astype(BF)

    each_place(put)


def scores_step(cols, chunk, begin, end, qt, kn, e_ref, inv_ref, sa, sb, ma):
    i = pl.program_id(0)

    @pl.when(i == 0)
    def _():
        m, _ = score_half(kn, qt[:, begin : begin + cols], sa, None, None, None, chunk, cols)
        ma[...] = jnp.broadcast_to(m, ma.shape)

    def q_block(b):
        return qt[:, pl.ds(pl.multiple_of(begin + b * cols, cols), cols)]

    def emit0(r, v):
        e_ref[r : r + chunk, 0:cols] = v

    def emit1(r, v):
        e_ref[r : r + chunk, cols : 2 * cols] = v

    mb, l0 = score_half(kn, q_block(2 * i + 1), sb, sa, ma[0:1, :], emit0, chunk, cols)
    nxt = jnp.minimum(2 * i + 2, (end - begin) // cols - 1)
    mn, l1 = score_half(kn, q_block(nxt), sa, sb, mb, emit1, chunk, cols)
    ma[...] = jnp.broadcast_to(mn, ma.shape)
    inv_ref[...] = jnp.broadcast_to(1.0 / jnp.concatenate([l0, l1], axis=1), (8, 2 * cols))


def scores_a_body(cols, chunk, x_ref, e_ref, inv_ref, qt, kn, kt_ref, vn_ref, sa, sb, ma):
    @pl.when(pl.program_id(0) == 0)
    def _():
        prepare(x_ref, qt, kn, kt_ref, vn_ref)

    scores_step(cols, chunk, 0, CUT, qt, kn, e_ref, inv_ref, sa, sb, ma)


def scores_b_body(cols, chunk, qt, kn, e_ref, inv_ref, sa, sb, ma):
    scores_step(cols, chunk, CUT, N, qt, kn, e_ref, inv_ref, sa, sb, ma)


def scores_call(body, name, size, more, operands, cols=256):
    return pl.pallas_call(
        body,
        grid=(size // cols // 2,),
        in_specs=[whole(*x.shape) for x in operands],
        out_specs=[
            pl.BlockSpec((N, 2 * cols), lambda i: (0, i)),
            pl.BlockSpec((8, 2 * cols), lambda i: (0, i)),
        ]
        + [whole(*shape) for shape in more],
        out_shape=[
            jax.ShapeDtypeStruct((N, size), BF),
            jax.ShapeDtypeStruct((8, size), F32),
        ]
        + [jax.ShapeDtypeStruct(shape, BF) for shape in more],
        scratch_shapes=[
            pltpu.VMEM((N, cols), F32),
            pltpu.VMEM((N, cols), F32),
            pltpu.VMEM((8, cols), F32),
        ],
        compiler_params=params(),
        cost_estimate=cost(2 * N * size * HD, 2 * size * N, N * size),
        name=name,
    )(*operands)


def scores_a(qkv):
    more = [(HD, N), (N, HD), (HD, N), (N, EXT)]
    return scores_call(functools.partial(scores_a_body, 256, 128), "scores_a", CUT, more, [qkv])


def scores_b(qt, kn):
    return scores_call(functools.partial(scores_b_body, 256, 128), "scores_b", N - CUT, [], [qt, kn])


CUT = 2048


def grads_block(k0, rows, e1, e2, inv1, inv2, qt, kt, vn, dot_t, dot_n, acc):
    v = vn[pl.ds(k0, rows), :]
    k = kt[:, pl.ds(k0, rows)]
    dv = dk = None
    for sl, e_ref, inv in ((slice(0, CUT), e1, inv1), (slice(CUT, N), e2, inv2)):
        e = e_ref[...]
        dp = dot(v, dot_t[:, sl], 1, 0)
        ds = (e.astype(F32) * dp * inv[0:1, :]).astype(BF)
        v_part = dot(e, dot_n[:, sl], 1, 1)
        k_part = dot(ds, qt[:, sl], 1, 1)
        dv = v_part if dv is None else dv + v_part
        dk = k_part if dk is None else dk + k_part
        acc[:, sl] += dot(k, ds, 1, 0)
    return dv.T.astype(BF), (dk * SCALE).T.astype(BF)


def grads_a_body(rows, x_ref, e1, e2, inv1, inv2, qt_ref, kt_ref, vn_ref, out_ref, dq_ref, dot_t, dot_n):
    i = pl.program_id(0)

    @pl.when(i == 0)
    def _():
        def side(s, small, sl):
            own = piece(x_ref, s, sl, 0, small).astype(F32)
            other = piece(x_ref, s ^ 1, sl, 1, small).astype(F32)
            return own, other

        def put(a, pieces):
            feats = []
            sums = []
            for s, small in pieces:
                own, other = side(s, small, slice(0, 48))
                first, second = (own, other) if s % 2 == 0 else (other, own)
                feats.append(jnp.concatenate([first[:HALF], second[:HALF]], axis=0))
                sums.append(own[HALF:] + jnp.concatenate([jnp.zeros((3, own.shape[1]), F32), other[HALF : HALF + 3], jnp.zeros((2, own.shape[1]), F32)], axis=0))
            f = joined(feats)
            t = joined(sums)
            dot_t[:, a : a + 128] = jnp.concatenate([f, t, jnp.zeros((8, 128), F32)], axis=0).astype(BF)
            inv = inv1[0:1, a : a + 128] if a < CUT else inv2[0:1, a - CUT : a - CUT + 128]
            dot_n[:, a : a + 128] = (f * inv).astype(BF)

        each_place(put)
        dq_ref[...] = jnp.zeros_like(dq_ref)

    k0 = pl.multiple_of(i * rows, 128)
    dv, dk = grads_block(
        k0, rows, e1, e2, inv1, inv2, qt_ref, kt_ref, vn_ref, dot_t, dot_n, dq_ref
    )
    for j in range(rows // BIG):
        out_ref[j, 0:HD, 0:BIG] = dv[:, j * BIG : (j + 1) * BIG]
        out_ref[j, 0:HD, BIG : 2 * BIG] = dk[:, j * BIG : (j + 1) * BIG]


def grads_a(dout, e1, e2, inv1, inv2, qt, kt, vn, rows=512):
    return pl.pallas_call(
        functools.partial(grads_a_body, rows),
        grid=(SRC * BIG // rows,),
        in_specs=[
            whole(SRC, 48, 384),
            pl.BlockSpec((rows, CUT), lambda i: (i, 0)),
            pl.BlockSpec((rows, N - CUT), lambda i: (i, 0)),
            whole(8, CUT),
            whole(8, N - CUT),
            whole(HD, N),
            whole(HD, N),
            whole(N, EXT),
        ],
        out_specs=[
            pl.BlockSpec((rows // BIG, HD, 2 * BIG), lambda i: (i, 0, 0)),
            whole(HD, N),
            whole(EXT, N),
            whole(HD, N),
        ],
        out_shape=[
            jax.ShapeDtypeStruct((SRC, HD, 2 * BIG), BF),
            jax.ShapeDtypeStruct((HD, N), F32),
            jax.ShapeDtypeStruct((EXT, N), BF),
            jax.ShapeDtypeStruct((HD, N), BF),
        ],
        compiler_params=params(),
        cost_estimate=cost(8 * N * SRC * BIG * HD, 18 * 10**6),
        name="grads_a",
    )(dout, e1, e2, inv1, inv2, qt, kt, vn)


def grads_b_body(rows, e1, e2, inv1, inv2, qt_ref, kt_ref, vn_ref, dot_t, dot_n, dq_ref, out_ref, acc):
    i = pl.program_id(0)
    base = SRC * BIG

    @pl.when(i == 0)
    def _():
        acc[...] = dq_ref[...]

    k0 = pl.multiple_of(base + i * rows, 128)
    dv, dk = grads_block(
        k0, rows, e1, e2, inv1, inv2, qt_ref, kt_ref, vn_ref, dot_t, dot_n, acc
    )
    for j in range(rows // SMALL):
        a = j * SMALL
        out_ref[i * (rows // SMALL) + j, 0:HD, :] = jnp.concatenate(
            [dv[:, a : a + SMALL], dk[:, a : a + SMALL]], axis=1
        )

    @pl.when(i == pl.num_programs(0) - 1)
    def _():
        for s in range(SRC):
            out_ref[s, HD : 2 * HD, :] = (acc[:, s * BIG : (s + 1) * BIG] * SCALE).astype(BF)
            a = base + s * SMALL
            b = acc[:, a : a + SMALL] * SCALE
            out_ref[s, 2 * HD : 2 * HD + HALF, :] = jnp.concatenate(
                [b[:HALF], b[HALF:]], axis=1
            ).astype(BF)


def grads_b(e1, e2, inv1, inv2, qt, kt, vn, dot_t, dot_n, dq, rows=512):
    off = SRC * BIG // rows
    return pl.pallas_call(
        functools.partial(grads_b_body, rows),
        grid=(SRC * SMALL // rows,),
        in_specs=[
            pl.BlockSpec((rows, CUT), lambda i: (i + off, 0)),
            pl.BlockSpec((rows, N - CUT), lambda i: (i + off, 0)),
            whole(8, CUT),
            whole(8, N - CUT),
            whole(HD, N),
            whole(HD, N),
            whole(N, EXT),
            whole(EXT, N),
            whole(HD, N),
            whole(HD, N),
        ],
        out_specs=whole(SRC, 200, 128),
        out_shape=jax.ShapeDtypeStruct((SRC, 200, 128), BF),
        scratch_shapes=[pltpu.VMEM((HD, N), F32)],
        compiler_params=params(),
        cost_estimate=cost(8 * N * SRC * SMALL * HD, 11 * 10**6),
        name="grads_b",
    )(e1, e2, inv1, inv2, qt, kt, vn, dot_t, dot_n, dq)


def patch_rows(ref, sl, lanes):
    return jnp.concatenate([ref[h, sl, lanes] for h in range(HEADS)], axis=0).T


def unpack_a_body(a_ref, dk_ref, dv_ref):
    dv_ref[0] = patch_rows(a_ref, slice(0, HD), slice(0, BIG))
    dk_ref[0] = patch_rows(a_ref, slice(0, HD), slice(BIG, 2 * BIG))


def unpack_a(a):
    shape = jax.ShapeDtypeStruct((1, TOK, D), BF)
    spec = pl.BlockSpec((1, BIG, D), lambda i: (0, 0, 0))
    return pl.pallas_call(
        unpack_a_body,
        grid=(1,),
        in_specs=[whole(HEADS, HD, 2 * BIG)],
        out_specs=[spec, spec],
        out_shape=[shape, shape],
        compiler_params=params(LESS),
        cost_estimate=cost(0, 2 * 10**6),
        name="unpack_a",
    )(a)


def unpack_b_body(at_ref, b_ref, w_own, w_oth, dk_in, dv_in, dq_ref, dk_ref, dv_ref, dw_ref):
    both = patch_rows(b_ref, slice(0, HD), slice(0, BIG))
    dv_ref[0] = both[:SMALL]
    dk_ref[0] = both[SMALL:]
    dq_ref[0, 0:BIG] = patch_rows(b_ref, slice(HD, 2 * HD), slice(0, BIG))
    tail = []
    for h in range(HEADS):
        t = b_ref[h, 2 * HD : 2 * HD + HALF, :].astype(F32)
        tail += [t[:, :SMALL], t[:, SMALL:]]
    dq_ref[0, BIG:TOK] = jnp.concatenate(tail, axis=0).T.astype(BF)
    c = at_ref[0]
    factor = 1.0 / float(16 * N) ** 0.5
    for ref, row in ((w_own, c), (w_oth, 1 - c)):
        dw_ref[pl.ds(pl.multiple_of(row * HALF, 8), HALF), :] = ref[...] * factor


def unpack_b(at, b, parts, dk, dv):
    shape = jax.ShapeDtypeStruct((1, TOK, D), BF)
    spec = pl.BlockSpec((1, SMALL, D), lambda i: (0, 2, 0))
    hbm = pl.BlockSpec(memory_space=pl.ANY)
    return pl.pallas_call(
        unpack_b_body,
        grid=(1,),
        in_specs=[pl.BlockSpec(memory_space=pltpu.SMEM), whole(HEADS, 200, 128)]
        + [whole(HALF, D)] * 2
        + [hbm, hbm],
        out_specs=[whole(1, TOK, D), spec, spec, whole(HD, D)],
        out_shape=[shape] * 3 + [jax.ShapeDtypeStruct((HD, D), F32)],
        input_output_aliases={4: 1, 5: 2},
        compiler_params=params(LESS),
        cost_estimate=cost(0, 3 * 10**6),
        name="unpack_b",
    )(at, b, *parts, dk, dv)


UP = [(i, (i + 1) % 8) for i in range(8)]
DOWN = [(i, (i - 1) % 8) for i in range(8)]


def body(query, keys, values, attn, d_block, w_out):
    c = lax.axis_index("c")
    yl = lax.axis_index("yl")
    z = lax.axis_index("z")
    swap = [(0, 1), (1, 0)]

    def exchange(x):
        return lax.all_to_all(x, SEQ, 0, 0, tiled=True)

    hold = lax.optimization_barrier

    def scalar(*i):
        return jnp.stack(i).astype(jnp.int32)

    def up(block):
        return lax.ppermute(block, "z", UP)

    def down(block):
        return lax.ppermute(block, "z", DOWN)

    w_half = lax.dynamic_slice_in_dim(w_out, c * HALF, HALF, 0)
    pair = jnp.stack([w_half, lax.ppermute(w_half, "yl", swap)])
    g_oth = lax.ppermute(d_block, "c", swap)
    packed = pack_qkv(query, keys, values)
    zs = [(z + o) % 8 for o in OFFSETS]
    ids = scalar(*[y * 8 + k for k in zs for y in (yl, 1 - yl)])
    pair, packed, g_oth, attn, ids = hold((pair, packed, g_oth, attn, ids))
    qkv = exchange(packed)
    f1, g1, attn = hold((up(pair), down(pair), attn))
    a_own, a_send = split_attn(scalar(c), attn)
    f2, g2, a_send = hold((up(f1), down(g1), a_send))
    a_oth = lax.ppermute(a_send, "c", swap)
    f3, g3, a_oth = hold((up(f2), down(g2), a_oth))
    keep, give, gx, ax = weight_share(scalar(yl), d_block, g_oth, a_own, a_oth)
    f4, give = hold((up(f3), give))
    came = lax.ppermute(give, "yl", swap)

    dout = out_grad(ids, [pair, f1, g1, f2, g2, f3, g3, f4], gx, ax)
    dout, qkv = hold((dout, qkv))
    dout = exchange(dout)

    e1, inv1, qt, kn, kt, vn = scores_a(qkv)
    came, qt, inv1 = hold((came, qt, inv1))
    part = (keep.astype(F32) + came.astype(F32)).astype(BF)
    part, dout, qt = hold((part, dout, qt))
    part = lax.all_to_all(part, "z", 0, 0, tiled=True)
    e2, inv2 = scores_b(qt, kn)
    first, dq, dot_t, dot_n = grads_a(dout, e1, e2, inv1, inv2, qt, kt, vn)
    first, part = hold((first, part))
    first = exchange(first)
    second = grads_b(e1, e2, inv1, inv2, qt, kt, vn, dot_t, dot_n, dq)
    mine = jnp.sum(part.astype(F32), axis=0)
    t = mine
    for k in range(1, 4):
        t = t + lax.ppermute(mine, "x", [(i, (i + k) % 4) for i in range(4)])
    second, t = hold((second, t))
    second = exchange(second)
    other = lax.ppermute(t, "yh", swap)
    other, d_keys, d_values = hold((other, *unpack_a(first)))
    u = t + other
    return unpack_b(scalar(c), second, [u, lax.ppermute(u, "c", swap)], d_keys, d_values)


def solution(mesh):
    finer = Mesh(mesh.devices.reshape(2, 4, 2, 2, 8), ("yh", "x", "c", "yl", "z"))
    rows = P(DP, SEQ, None)
    weight = P(DP, None)
    return jax.shard_map(
        body,
        mesh=finer,
        in_specs=(rows,) * 5 + (weight,),
        out_specs=(rows,) * 3 + (weight,),
        check_vma=False,
    )
```
